32 devices in a mesh: groups: 2 (over x), seq: 16 (over z, y, core).
Axes of the slice: x: 2, y: 2, z: 4, core: 2. Of those that a mesh axis runs over, the one named last changes fastest.
Arguments:
- queries: bfloat16 [4096, 1024], P(('groups', 'seq')), parts along dimension 0, may hold values from -6 to 6
- key_rows: bfloat16 [4096, 1024], P(('groups', 'seq')), parts along dimension 0, may hold values from -6 to 6
- value_rows: bfloat16 [4096, 1024], P(('groups', 'seq')), parts along dimension 0, may hold values from -6 to 6
- strength: float32 [4096, 8], P(('groups', 'seq')), parts along dimension 0, may hold values from 0 to 1, as said below
- conv_weight: bfloat16 [3, 4, 1024], replicated, may hold values from -3 to 3
- out_gain: float32 [128], replicated, may hold values from 0.5 to 1.5
Outputs:
- mixed: bfloat16 [4096, 1024], P(('groups', 'seq')), parts along dimension 0
The draws below stay inside these ranges and needn't reach their ends.
There are 2 independent parts, one for each index of `groups`. The reference program is written for one: setup_inputs(seed, part) draws one part's arguments, and reference() takes and returns one part's arrays. A program takes and returns all parts, laid end to end along the dimension named above; an argument that names none is the same for every part. Nothing has to cross between parts.
Inputs may be any that keep to these rules, and one draw needn't show every extreme that they name: A write strength of each token and head, positive and at most one.
All inputs are finite; a program needn't handle non-finite values.
Results may differ from the reference program's by a relative error of at most 0.001.
Values may be sent and summed in bfloat16 or wider, within the bound.
No kernel may reach another device: no remote copies, remote signals or barrier semaphores. Data moves between devices by JAX's collectives and lax.ppermute only.
A program may use at most 192 MiB of HBM per device.

```python
import jax
import jax.numpy as jnp
from jax import lax

HEAD_COUNT = 8
DK = 128
CONV = 4
SEQUENCE_TOKENS = 2048


def draw_strength(key, part):
    key_vectors = jax.random.split(jax.random.fold_in(key, 7103), 6)
    order = jax.random.permutation(key_vectors[0], HEAD_COUNT)
    slow_heads = order < HEAD_COUNT // 2
    slow_base = jax.random.uniform(key_vectors[1], (HEAD_COUNT,), jnp.float32, 0.2, 1.0) * DK / SEQUENCE_TOKENS
    fast_base = jnp.exp(jax.random.uniform(key_vectors[2], (HEAD_COUNT,), jnp.float32, jnp.log(0.3), jnp.log(0.9)))
    base = jnp.where(slow_heads, slow_base, fast_base)
    factor = jnp.exp(jax.random.uniform(key_vectors[3], (SEQUENCE_TOKENS, HEAD_COUNT), jnp.float32, jnp.log(0.5), jnp.log(1.5)))
    decay_rates = jnp.minimum(base[None, :] * factor, 1.0)
    token_positions = jax.random.randint(key_vectors[4], (8,), 0, SEQUENCE_TOKENS)
    surge_events = jnp.zeros((SEQUENCE_TOKENS,), jnp.float32).at[token_positions].set(1.0)
    surge_level = jax.random.uniform(key_vectors[5], (SEQUENCE_TOKENS, HEAD_COUNT), jnp.float32, 0.4, 0.7)
    return jnp.where(surge_events[:, None] > 0.0, jnp.maximum(decay_rates, surge_level), decay_rates)


def levels(rng, extent, cuts, low, top_value):
    factor_of, own = 1.0, jax.random.fold_in(rng, 6)
    for axis_at, shards_of in cuts:
        draws = jnp.exp(jax.random.uniform(jax.random.fold_in(own, axis_at), (shards_of,), jnp.float32, low / len(cuts), top_value / len(cuts)))
        factor_of = factor_of * jnp.repeat(draws, extent[axis_at] // shards_of).reshape([-1 if axis == axis_at else 1 for axis in range(len(extent))])
    return factor_of


def bell_draw(rng, extent, scale, reach, cuts=(), held_as=jnp.bfloat16):
    entries = scale * jax.random.normal(rng, extent, jnp.float32)
    if cuts:
        entries = entries * levels(rng, extent, cuts, -0.22, 0.18)
    return jnp.clip(entries, -reach, reach).astype(held_as)


def setup_inputs(seed: int = 0, part: int = 0) -> dict:
    arg_keys = jax.random.split(jax.random.key(seed), 7)
    part_keys = jax.random.split(jax.random.fold_in(arg_keys[6], part), 7)
    queries = bell_draw(part_keys[0], (SEQUENCE_TOKENS, HEAD_COUNT * DK), 1.0, 6.0, ((0, 16),))
    key_rows = bell_draw(part_keys[1], (SEQUENCE_TOKENS, HEAD_COUNT * DK), 1.0, 6.0, ((0, 16),))
    value_rows = bell_draw(part_keys[2], (SEQUENCE_TOKENS, HEAD_COUNT * DK), 1.0, 6.0, ((0, 16),))
    strength = draw_strength(jax.random.fold_in(jax.random.fold_in(arg_keys[6], part), 71), part)
    conv_weight = bell_draw(arg_keys[4], (3, CONV, HEAD_COUNT * DK), CONV ** -0.5, 3.0)
    out_gain = jnp.clip(1.0 + 0.1 * jax.random.normal(arg_keys[5], (DK,), jnp.float32), 0.5, 1.5)
    return {"queries": queries, "key_rows": key_rows, "value_rows": value_rows, "strength": strength, "conv_weight": conv_weight, "out_gain": out_gain}


def convolve(source, kernel):
    width = CONV - 1
    extended = jnp.concatenate([jnp.zeros((width, source.shape[1]), jnp.float32), source.astype(jnp.float32)], axis=0)
    kernel = kernel.astype(jnp.float32)
    summed = extended[0:SEQUENCE_TOKENS] * kernel[0]
    for offset in range(1, width + 1):
        summed = summed + extended[offset:offset + SEQUENCE_TOKENS] * kernel[offset]
    return jax.nn.silu(summed).reshape(SEQUENCE_TOKENS, HEAD_COUNT, DK)

def unit_rows(values):
    return values / jnp.sqrt(lax.optimization_barrier(jnp.sum(values * values, axis=-1, keepdims=True)) + 1e-06)

def reference(queries, key_rows, value_rows, strength, conv_weight, out_gain):
    highest = lax.Precision.HIGHEST
    query_heads = unit_rows(convolve(queries, conv_weight[0]))
    key_heads = unit_rows(convolve(key_rows, conv_weight[1]))
    value_heads = convolve(value_rows, conv_weight[2])

    def advance(memory, pieces):
        query_now, key_now, value_now, rate_now = pieces
        predicted = jnp.einsum('hd,hde->he', key_now, memory, precision=highest)
        memory = memory + (rate_now[:, None] * key_now)[:, :, None] * (value_now - predicted)[:, None, :]
        output = jnp.einsum('hd,hde->he', query_now, memory, precision=highest)
        return (memory, output)
    start = jnp.zeros((HEAD_COUNT, DK, DK), jnp.float32)
    final, outputs = lax.scan(advance, start, (query_heads, key_heads, value_heads, strength.astype(jnp.float32)))
    normed = outputs * lax.rsqrt(lax.optimization_barrier(jnp.mean(outputs * outputs, axis=-1, keepdims=True)) + 1e-05) * out_gain
    return normed.astype(jnp.bfloat16).reshape(SEQUENCE_TOKENS, HEAD_COUNT * DK)
```

```python
import functools

import jax
import jax.numpy as jnp
from jax import lax
from jax.experimental import pallas as pl
from jax.experimental.pallas import tpu as pltpu
from jax.sharding import PartitionSpec as P

EXTRA = 16
F32 = jnp.float32
BF16 = jnp.bfloat16


def split(x):
    high = x.astype(BF16)
    return high, (x - high.astype(F32)).astype(BF16)


def left(parts):
    return jnp.concatenate(parts, axis=1)


def right(parts):
    both = jnp.concatenate(parts, axis=1)
    return jnp.concatenate([both, both], axis=0)


def product(lhs, rhs):
    both = lax.dot_general(lhs, rhs, (((1,), (0,)), ((), ())), preferred_element_type=F32)
    half = both.shape[1] // 2
    return both[:, :half] + both[:, half:]


def product_t(a, b):
    dims = (((1,), (1,)), ((), ()))
    lhs = jnp.concatenate(a, axis=1)
    rhs_high = jnp.concatenate([b[0], b[0]], axis=1)
    rhs_low = jnp.concatenate([b[1], b[1]], axis=1)
    both = lax.dot_general(
        lhs, jnp.concatenate([rhs_high, rhs_low], axis=0), dims, preferred_element_type=F32
    )
    half = both.shape[1] // 2
    return both[:, :half] + both[:, half:]


def rows_kernel(width, raw_ref, taps_ref, local_ref, carry_ref, final_ref, ext_ref):
    chunks, _, depth = raw_ref.shape
    span = (raw_ref.shape[1] - EXTRA) // 3
    row = lax.broadcasted_iota(jnp.int32, (span, span), 0)
    col = lax.broadcasted_iota(jnp.int32, (span, span), 1)
    eye = (row == col).astype(F32)

    def activated(c, index, extra):
        base = index * 1
        ext_ref[base, 8 - width : 8, :] = extra[index * width : (index + 1) * width]
        ext_ref[base, 8 : 8 + span, :] = raw_ref[c, index * span : (index + 1) * span, :].astype(F32)
        total = None
        for tap in range(width + 1):
            term = ext_ref[base, 8 - width + tap : 8 - width + tap + span, :] * taps_ref[
                index * (width + 1) + tap : index * (width + 1) + tap + 1, :
            ]
            total = term if total is None else total + term
        return total / (1.0 + jnp.exp(-total))

    def unit(x):
        return x * lax.rsqrt(jnp.sum(x * x, axis=-1, keepdims=True) + 1e-06)

    state = None
    stage = []
    for c in range(chunks):
        extra = raw_ref[c, 3 * span :, :].astype(F32)
        query = unit(activated(c, 0, extra))
        key = unit(activated(c, 1, extra))
        value = activated(c, 2, extra)
        at = 3 * width
        rate_row = extra[at : at + 1] + extra[at + 1 : at + 2] + extra[at + 2 : at + 3]
        rate = jnp.sum(eye * rate_row, axis=1, keepdims=True)
        key_parts = split(key)
        scores = jnp.where(row >= col, product_t(split(query), key_parts), 0.0)
        lower = jnp.where(row > col, rate * product_t(key_parts, key_parts), 0.0)
        stage.append((query, key, value, rate, scores, lower))
    inverses = []
    for c in range(chunks):
        lower = stage[c][5]
        inverses.append(eye - jnp.where((row ^ col) == 1, lower, 0.0))
    size = 2
    while size < span:
        for c in range(chunks):
            pick = ((row ^ col) < 2 * size) & ((row & size) != (col & size))
            block = jnp.where(pick, stage[c][5], 0.0)
            parts = split(inverses[c])
            inner = product(left(split(block)), right(parts))
            inverses[c] = inverses[c] - product(left(parts), right(split(inner)))
        size *= 2
    for c in range(chunks):
        query, key, value, rate, scores, lower = stage[c]
        both = jnp.concatenate([rate * key, rate * value], axis=1)
        solved = product(left(split(inverses[c])), right(split(both)))
        solved = right(split(solved))
        moved = product(left(split(key.T)), solved)
        shown = product(left(split(scores)), solved)
        seen = query - shown[:, :depth]
        if c == 0:
            local_ref[c] = shown[:, depth:]
            carry_ref[c] = seen
            state = jnp.concatenate([eye - moved[:, :depth], moved[:, depth:]], axis=1)
        else:
            state_parts = right(split(state))
            out = product(left(split(seen)), state_parts)
            carry_ref[c] = out[:, :depth]
            local_ref[c] = shown[:, depth:] + out[:, depth:]
            through = product(left(split(eye - moved[:, :depth])), state_parts)
            state = jnp.concatenate([through[:, :depth], through[:, depth:] + moved[:, depth:]], axis=1)
    final_ref[0] = state[:, :depth]
    final_ref[1] = state[:, depth:]


def finish_kernel(local_ref, carry_ref, memory_ref, gain_ref, out_ref):
    chunks = local_ref.shape[0]
    memory = right(split(memory_ref[...]))
    gain = gain_ref[...]
    for c in range(chunks):
        output = local_ref[c] + product(left(split(carry_ref[c])), memory)
        scale = lax.rsqrt(jnp.mean(output * output, axis=-1, keepdims=True) + 1e-05)
        out_ref[c] = (output * scale * gain).astype(BF16)


def compose(later, earlier):
    join = functools.partial(jnp.einsum, "ij,jk->ik", precision=lax.Precision.HIGHEST)
    return jnp.stack([join(later[0], earlier[0]), join(later[0], earlier[1]) + later[1]])


def shards(queries, key_rows, value_rows, strength, conv_weight, out_gain):
    taps = conv_weight.shape[1]
    width = taps - 1
    span, heads = strength.shape
    depth = queries.shape[1] // heads
    count = lax.axis_size("seq")
    place = lax.axis_index("seq")
    blocks = count // heads
    assert blocks * heads == count
    groups = [[b * heads + h for h in range(heads)] for b in range(blocks)]
    block, head = place // heads, place % heads

    def by_head(x):
        return x.reshape(-1, heads, depth).transpose(1, 0, 2)

    tails = jnp.concatenate([queries[-width:], key_rows[-width:], value_rows[-width:]])
    tails = lax.ppermute(tails, "seq", [(i, i + 1) for i in range(count - 1)])
    high = lax.reduce_precision(strength, 8, 7)
    rest = strength - high
    middle = lax.reduce_precision(rest, 8, 7)
    rates = jnp.stack([high.T, middle.T, (rest - middle).T], axis=1).astype(BF16)
    pad = jnp.zeros((heads, EXTRA - 3 * width - 3, depth), BF16)
    payload = jnp.concatenate(
        [by_head(queries), by_head(key_rows), by_head(value_rows), by_head(tails), rates, pad], axis=1
    )
    raw = lax.all_to_all(payload, "seq", 0, 0, axis_index_groups=groups, tiled=True)
    kernel_taps = lax.dynamic_slice_in_dim(
        conv_weight.reshape(3 * taps, heads * depth), head * depth, depth, 1
    ).astype(F32)

    whole = pl.BlockSpec(memory_space=pltpu.VMEM)
    local, carry, final = pl.pallas_call(
        functools.partial(rows_kernel, width),
        out_shape=(
            jax.ShapeDtypeStruct((heads, span, depth), F32),
            jax.ShapeDtypeStruct((heads, span, depth), F32),
            jax.ShapeDtypeStruct((2, depth, depth), F32),
        ),
        in_specs=[whole] * 2,
        out_specs=[whole] * 3,
        scratch_shapes=[pltpu.VMEM((3, span + 8, depth), F32)],
        name="rows",
    )(raw, kernel_taps)

    ring = [(i, (i + heads) % count) for i in range(count)]
    if blocks == 2:
        memory = lax.ppermute(final[1], "seq", ring)
        memory = jnp.where(block > 0, memory, 0.0)
    else:
        start = jnp.stack([jnp.eye(depth, dtype=F32), jnp.zeros((depth, depth), F32)])
        arrived = lax.ppermute(final, "seq", ring)
        prefix = jnp.where(block > 0, arrived, start)
        step = 1
        while step < blocks - 1:
            shift = [(i, (i + step * heads) % count) for i in range(count)]
            arrived = lax.ppermute(prefix, "seq", shift)
            prefix = jnp.where(block >= step, compose(prefix, arrived), prefix)
            step *= 2
        memory = prefix[1]

    mixed = pl.pallas_call(
        finish_kernel,
        out_shape=jax.ShapeDtypeStruct((heads, span, depth), BF16),
        in_specs=[whole] * 4,
        out_specs=whole,
        name="finish",
    )(local, carry, memory, out_gain.reshape(1, depth))
    mixed = lax.all_to_all(mixed, "seq", 0, 0, axis_index_groups=groups, tiled=True)
    return mixed.transpose(1, 0, 2).reshape(span, heads * depth)


def solution(mesh):
    placed = (
        P(("groups", "seq"), None),
        P(("groups", "seq"), None),
        P(("groups", "seq"), None),
        P(("groups", "seq"), None),
        P(),
        P(),
    )
    return jax.shard_map(
        shards, mesh=mesh, in_specs=placed, out_specs=P(("groups", "seq"), None), check_vma=False
    )
```

```python
import functools

import jax
import jax.numpy as jnp
from jax import lax
from jax.experimental import pallas as pl
from jax.experimental.pallas import tpu as pltpu
from jax.sharding import PartitionSpec as P

EXTRA = 16
VMEM_LIMIT = 24 * 1024 * 1024
F32 = jnp.float32
BF16 = jnp.bfloat16


def split(x):
    high = x.astype(BF16)
    return high, (x - high.astype(F32)).astype(BF16)


def left(parts):
    return jnp.concatenate(parts, axis=1)


def right(parts):
    both = jnp.concatenate(parts, axis=1)
    return jnp.concatenate([both, both], axis=0)


def product(lhs, rhs):
    both = lax.dot_general(lhs, rhs, (((1,), (0,)), ((), ())), preferred_element_type=F32)
    half = both.shape[1] // 2
    return both[:, :half] + both[:, half:]


def product_t(a, b):
    dims = (((1,), (1,)), ((), ()))
    lhs = jnp.concatenate(a, axis=1)
    rhs_high = jnp.concatenate([b[0], b[0]], axis=1)
    rhs_low = jnp.concatenate([b[1], b[1]], axis=1)
    both = lax.dot_general(
        lhs, jnp.concatenate([rhs_high, rhs_low], axis=0), dims, preferred_element_type=F32
    )
    half = both.shape[1] // 2
    return both[:, :half] + both[:, half:]


def pack_kernel(width, at_ref, q_ref, k_ref, v_ref, tail_ref, rate_ref, *refs):
    pieces, parts_ref, tile_ref = refs[:-2], refs[-2], refs[-1]
    span, heads = rate_ref.shape
    depth = q_ref.shape[1] // heads
    rate = rate_ref[...].T
    for part in range(3):
        high = rate.astype(BF16).astype(F32)
        parts_ref[part] = high
        rate = rate - high
    tile_ref[...] = jnp.zeros_like(tile_ref)
    for slot in range(heads):
        head = at_ref[0] ^ slot
        lanes = pl.ds(pl.multiple_of(head * depth, depth), depth)
        for index, source in enumerate((q_ref, k_ref, v_ref)):
            pieces[slot][index * span : (index + 1) * span, :] = source[:, lanes]
        tile_ref[slot, : 3 * width, :] = tail_ref[: 3 * width, lanes].astype(F32)
        for part in range(3):
            tile_ref[slot, 3 * width + part : 3 * width + part + 1, :] = parts_ref[
                part, pl.ds(head, 1), :
            ]
        pieces[slot][3 * span :, :] = tile_ref[slot].astype(BF16)


def rows_kernel(width, second, at_ref, taps_ref, *refs):
    if second:
        early_p_ref, early_n_ref = refs[:2]
        refs = refs[2:]
    count = len(refs) - (6 if second else 4) - 2
    raws, refs = refs[:count], refs[count:]
    local_ref, carry_ref, final_p_ref, final_n_ref = refs[:4]
    if second:
        block_p_ref, block_n_ref = refs[4:6]
    ext_ref, step_ref = refs[-2:]
    depth = raws[0].shape[1]
    span = (raws[0].shape[0] - EXTRA) // 3
    row = lax.broadcasted_iota(jnp.int32, (span, span), 0)
    col = lax.broadcasted_iota(jnp.int32, (span, span), 1)
    eye = (row == col).astype(F32)
    taps = taps_ref[:, pl.ds(pl.multiple_of(at_ref[0] * depth, depth), depth)].astype(F32)

    def activated(c, index, extra):
        ext_ref[index, 8 - width : 8, :] = extra[index * width : (index + 1) * width]
        ext_ref[index, 8 : 8 + span, :] = raws[c][index * span : (index + 1) * span, :].astype(F32)
        total = None
        for tap in range(width + 1):
            at = index * (width + 1) + tap
            term = ext_ref[index, 8 - width + tap : 8 - width + tap + span, :] * taps[at : at + 1]
            total = term if total is None else total + term
        return total / (1.0 + jnp.exp(-total))

    def unit(x):
        return x * lax.rsqrt(jnp.sum(x * x, axis=-1, keepdims=True) + 1e-06)

    stage = []
    for c in range(count):
        extra = raws[c][3 * span :, :].astype(F32)
        query = unit(activated(c, 0, extra))
        key = unit(activated(c, 1, extra))
        value = activated(c, 2, extra)
        at = 3 * width
        rate_row = extra[at : at + 1] + extra[at + 1 : at + 2] + extra[at + 2 : at + 3]
        rate = jnp.sum(eye * rate_row, axis=1, keepdims=True)
        key_parts = split(key)
        scores = jnp.where(row >= col, product_t(split(query), key_parts), 0.0)
        lower = jnp.where(row > col, rate * product_t(key_parts, key_parts), 0.0)
        stage.append((query, key, value, rate, scores, lower))
    inverses = []
    for c in range(count):
        lower = stage[c][5]
        inverses.append(eye - jnp.where((row ^ col) == 1, lower, 0.0))
    size = 2
    while size < span:
        for c in range(count):
            pick = ((row ^ col) < 2 * size) & ((row & size) != (col & size))
            block = jnp.where(pick, stage[c][5], 0.0)
            parts = split(inverses[c])
            inner = product(left(split(block)), right(parts))
            inverses[c] = inverses[c] - product(left(parts), right(split(inner)))
        size *= 2
    for c in range(count):
        query, key, value, rate, scores, lower = stage[c]
        both = jnp.concatenate([rate * key, rate * value], axis=1)
        solved = product(left(split(inverses[c])), right(split(both)))
        solved = right(split(solved))
        moved = product(left(split(key.T)), solved)
        shown = product(left(split(scores)), solved)
        local_ref[c] = shown[:, depth:]
        carry_ref[c] = query - shown[:, :depth]
        step_ref[c, :, :depth] = eye - moved[:, :depth]
        step_ref[c, :, depth:] = moved[:, depth:]
    for c in range(count):
        slot = (at_ref[0] & (count - 1)) ^ c
        if c == 0:
            state = step_ref[slot]
        else:
            parts = right(split(state))
            out = product(left(split(carry_ref[slot])), parts)
            carry_ref[slot] = out[:, :depth]
            local_ref[slot] += out[:, depth:]
            through = product(left(split(step_ref[slot, :, :depth])), parts)
            state = jnp.concatenate(
                [through[:, :depth], through[:, depth:] + step_ref[slot, :, depth:]], axis=1
            )
    final_p_ref[...] = state[:, :depth]
    final_n_ref[...] = state[:, depth:]
    if second:
        swap = (at_ref[0] & count) != 0
        early = jnp.concatenate([early_p_ref[...], early_n_ref[...]], axis=1)
        first = jnp.where(swap, state, early)
        last = jnp.where(swap, early, state)
        through = product(left(split(last[:, :depth])), right(split(first)))
        block_p_ref[...] = through[:, :depth]
        block_n_ref[...] = through[:, depth:] + last[:, depth:]


def finish_kernel(at_ref, local_a, carry_a, p_a, n_a, local_b, carry_b, p_b, n_b, memory_ref, gain_ref, *outs):
    count = local_a.shape[0]
    swap = (at_ref[0] & count) != 0
    memory = jnp.where(at_ref[1] > 0, memory_ref[...], 0.0)
    parts = right(split(memory))
    half_p = jnp.where(swap, p_b[...], p_a[...])
    half_n = jnp.where(swap, n_b[...], n_a[...])
    middle = product(left(split(half_p)), parts) + half_n
    gain = gain_ref[...]
    for base, local_ref, carry_ref, state in (
        (0, local_a, carry_a, jnp.where(swap, middle, memory)),
        (count, local_b, carry_b, jnp.where(swap, memory, middle)),
    ):
        state_parts = right(split(state))
        for c in range(count):
            output = local_ref[c] + product(left(split(carry_ref[c])), state_parts)
            scale = lax.rsqrt(jnp.mean(output * output, axis=-1, keepdims=True) + 1e-05)
            outs[base + c][...] = (output * scale * gain).astype(BF16)


def unpack_kernel(at_ref, *refs):
    out_ref = refs[-1]
    for slot, piece in enumerate(refs[:-1]):
        depth = piece.shape[1]
        lanes = pl.ds(pl.multiple_of((at_ref[0] ^ slot) * depth, depth), depth)
        out_ref[:, lanes] = piece[...]


def compose(later, earlier):
    join = functools.partial(jnp.einsum, "ij,jk->ik", precision=lax.Precision.HIGHEST)
    return jnp.stack([join(later[0], earlier[0]), join(later[0], earlier[1]) + later[1]])


WHOLE = pl.BlockSpec(memory_space=pltpu.VMEM)
SCALAR = pl.BlockSpec(memory_space=pltpu.SMEM)


def call(kernel, name, args, outs, scratch=(), several=True):
    shapes = [jax.ShapeDtypeStruct(shape, dtype) for shape, dtype in outs]
    return pl.pallas_call(
        kernel,
        out_shape=shapes if several else shapes[0],
        in_specs=[SCALAR] + [WHOLE] * (len(args) - 1),
        out_specs=[WHOLE] * len(shapes) if several else WHOLE,
        scratch_shapes=scratch,
        compiler_params=pltpu.CompilerParams(vmem_limit_bytes=VMEM_LIMIT),
        name=name,
    )(*args)


def exchange(pieces, heads, count):
    arrived = [pieces[0]]
    for slot in range(1, heads):
        pairs = [(i, i ^ slot) for i in range(count)]
        arrived.append(lax.ppermute(pieces[slot], "seq", pairs))
    return arrived


def shards(queries, key_rows, value_rows, strength, conv_weight, out_gain):
    taps = conv_weight.shape[1]
    width = taps - 1
    span, heads = strength.shape
    depth = queries.shape[1] // heads
    count = lax.axis_size("seq")
    place = lax.axis_index("seq")
    blocks = count // heads
    assert blocks * heads == count and heads & (heads - 1) == 0 and span == depth
    block, head = place // heads, place % heads
    at = jnp.stack([head, block]).astype(jnp.int32)
    square = (depth, depth)

    tails = jnp.concatenate([queries[-width:], key_rows[-width:], value_rows[-width:]])
    tails = lax.ppermute(tails, "seq", [(i, i + 1) for i in range(count - 1)])
    pieces = call(
        functools.partial(pack_kernel, width),
        "pack",
        (at, queries, key_rows, value_rows, tails, strength),
        [((3 * span + EXTRA, depth), BF16)] * heads,
        [pltpu.VMEM((3, heads, depth), F32), pltpu.VMEM((heads, EXTRA, depth), F32)],
    )
    raws = exchange(pieces, heads, count)
    half = heads // 2
    taps_flat = conv_weight.reshape(3 * taps, heads * depth)
    scratch = [pltpu.VMEM((3, span + 8, depth), F32), pltpu.VMEM((half, depth, 2 * depth), F32)]
    wide = [((half, span, depth), F32)] * 2
    first = call(
        functools.partial(rows_kernel, width, False),
        "rows_near",
        (at, taps_flat, *raws[:half]),
        wide + [(square, F32)] * 2,
        scratch,
    )
    second = call(
        functools.partial(rows_kernel, width, True),
        "rows_far",
        (at, taps_flat, first[2], first[3], *raws[half:]),
        wide + [(square, F32)] * 4,
        scratch,
    )

    ring = [(i, (i + heads) % count) for i in range(count)]
    if blocks <= 2:
        memory = lax.ppermute(second[5], "seq", ring)
    else:
        start = jnp.stack([jnp.eye(depth, dtype=F32), jnp.zeros(square, F32)])
        arrived = lax.ppermute(jnp.stack([second[4], second[5]]), "seq", ring)
        prefix = jnp.where(block > 0, arrived, start)
        step = 1
        while step < blocks - 1:
            shift = [(i, (i + step * heads) % count) for i in range(count)]
            arrived = lax.ppermute(prefix, "seq", shift)
            prefix = jnp.where(block >= step, compose(prefix, arrived), prefix)
            step *= 2
        memory = prefix[1]

    mixed = call(
        finish_kernel,
        "finish",
        (at, *first[:4], *second[:4], memory, out_gain.reshape(1, depth)),
        [((span, depth), BF16)] * heads,
    )
    mixed = exchange(mixed, heads, count)
    return call(unpack_kernel, "unpack", (at, *mixed), [((span, heads * depth), BF16)], several=False)


def solution(mesh):
    placed = (
        P(("groups", "seq"), None),
        P(("groups", "seq"), None),
        P(("groups", "seq"), None),
        P(("groups", "seq"), None),
        P(),
        P(),
    )
    return jax.shard_map(
        shards, mesh=mesh, in_specs=placed, out_specs=P(("groups", "seq"), None), check_vma=False
    )
```

```python
import functools

import jax
import jax.numpy as jnp
from jax import lax
from jax.experimental import pallas as pl
from jax.experimental.pallas import tpu as pltpu
from jax.sharding import PartitionSpec as P

EXTRA = 16
VMEM_LIMIT = 24 * 1024 * 1024
VMEM_ALL = 67043328
F32 = jnp.float32
BF16 = jnp.bfloat16


def pair(x):
    high = x.astype(BF16)
    return jnp.concatenate([high, (x - high.astype(F32)).astype(BF16)], axis=1)


def product(lhs, rhs):
    both = jnp.dot(lhs, jnp.concatenate([rhs, rhs], axis=0), preferred_element_type=F32)
    half = both.shape[1] // 2
    return both[:, :half] + both[:, half:]


def product_t(lhs, rhs):
    k = rhs.shape[1] // 2
    high, low = rhs[:, :k], rhs[:, k:]
    rhs = jnp.concatenate(
        [jnp.concatenate([high, high], axis=1), jnp.concatenate([low, low], axis=1)], axis=0
    )
    both = lax.dot_general(lhs, rhs, (((1,), (1,)), ((), ())), preferred_element_type=F32)
    half = both.shape[1] // 2
    return both[:, :half] + both[:, half:]


def pack_kernel(width, q_hbm, k_hbm, v_hbm, rate_ref, others_ref, tail_ref, rates_ref, *scratch):
    q_ref, k_ref, v_ref, parts_ref, tile_ref, sems = scratch
    heads, span = rate_ref.shape
    depth = q_ref.shape[1] // heads
    copies = [
        pltpu.make_async_copy(q_hbm, q_ref, sems.at[0]),
        pltpu.make_async_copy(k_hbm.at[span - EXTRA :, :], k_ref, sems.at[1]),
        pltpu.make_async_copy(v_hbm, v_ref, sems.at[2]),
    ]
    for copy in copies:
        copy.start()
    rate = rate_ref[...]
    for part in range(3):
        high = rate.astype(BF16).astype(F32)
        parts_ref[part] = high
        rate = rate - high
    tile_ref[...] = jnp.zeros_like(tile_ref)
    for head in range(heads):
        lanes = slice(head * depth, (head + 1) * depth)
        for part in range(3):
            at = 3 * width + part
            tile_ref[at : at + 1, lanes] = parts_ref[part, head : head + 1, :]
    rates_ref[...] = tile_ref[...].astype(BF16)
    tile_ref[...] = jnp.zeros_like(tile_ref)
    for copy in copies:
        copy.wait()
    for index, source in enumerate((q_ref, k_ref, v_ref)):
        tile_ref[index * width : (index + 1) * width, :] = source[source.shape[0] - width :, :].astype(F32)
    tail_ref[...] = tile_ref[...].astype(BF16)
    for head in range(heads):
        lanes = slice(head * depth, (head + 1) * depth)
        others_ref[head, :span, :] = v_ref[:, lanes]
        others_ref[head, span:, :] = q_ref[:, lanes]


def halo_kernel(tail_ref, rates_ref, rows_ref, keys_ref):
    heads, rows, depth = keys_ref.shape
    span = rows - EXTRA
    for head in range(heads):
        lanes = slice(head * depth, (head + 1) * depth)
        keys_ref[head, :span, :] = rows_ref[:, lanes]
        keys_ref[head, span:, :] = tail_ref[:, lanes] + rates_ref[:, lanes]


def head_taps(at_ref, taps_ref, depth):
    return taps_ref[:, pl.ds(pl.multiple_of(at_ref[0] * depth, depth), depth)].astype(F32)


def activated(rows, halo, taps, ext_ref):
    span, width = rows.shape[0], halo.shape[0]
    ext_ref[8 - width : 8, :] = halo
    ext_ref[8 : 8 + span, :] = rows.astype(F32)
    total = ext_ref[8 - width : 8 - width + span, :] * taps[:1]
    for tap in range(1, width + 1):
        total += ext_ref[8 - width + tap : 8 - width + tap + span, :] * taps[tap : tap + 1]
    return total / (1.0 + jnp.exp(-total))


def unit(x):
    return x * lax.rsqrt(jnp.sum(x * x, axis=-1, keepdims=True) + 1e-06)


def grids(span):
    row = lax.broadcasted_iota(jnp.int32, (span, span), 0)
    col = lax.broadcasted_iota(jnp.int32, (span, span), 1)
    return row, col, (row == col).astype(F32)


def scan_plan(chunks):
    plan, reach = [], 1
    while reach < chunks:
        plan.append([(c, (c // reach) * reach - 1) for c in range(chunks) if c // reach % 2])
        reach *= 2
    return plan


def keys_kernel(width, at_ref, taps_ref, raw_ref, key_ref, mix_ref, show_ref, extra_ref, factor_ref, through_ref, ext_ref, run_ref):
    chunks, rows, depth = raw_ref.shape
    span = rows - EXTRA
    row, col, eye = grids(span)
    taps = head_taps(at_ref, taps_ref, depth)[width + 1 : 2 * (width + 1)]
    lowers, inverses, rates, turned = [], [], [], []
    for c in range(chunks):
        extra = raw_ref[c, span:, :].astype(F32)
        extra_ref[c] = raw_ref[c, span:, :]
        key = unit(activated(raw_ref[c, :span, :], extra[width : 2 * width], taps, ext_ref.at[c]))
        at = 3 * width
        rates.append(extra[at : at + 1] + extra[at + 1 : at + 2] + extra[at + 2 : at + 3])
        rate = jnp.sum(eye * rates[c], axis=1, keepdims=True)
        key_pair = pair(key)
        key_ref[c] = key_pair
        turned.append(pair(key.T))
        lowers.append(jnp.where(row > col, rate * product_t(key_pair, key_pair), 0.0))
        inverses.append(eye - jnp.where((row ^ col) == 1, lowers[c], 0.0))
    size = 2
    while size < span:
        pick = ((row ^ col) < 2 * size) & ((row & size) != (col & size))
        for c in range(chunks):
            inverse = pair(inverses[c])
            inner = product(pair(jnp.where(pick, lowers[c], 0.0)), inverse)
            inverses[c] = inverses[c] - product(inverse, pair(inner))
        size *= 2
    for c in range(chunks):
        mix = pair(inverses[c] * rates[c])
        mix_ref[c] = mix
        show = pair(product(turned[c], mix))
        show_ref[c] = show
        run_ref[c] = pair(eye - product(show, key_ref[c]))
    at = 0
    for level in scan_plan(chunks):
        for c, earlier in level:
            factor_ref[at] = run_ref[c]
            at += 1
            if at < factor_ref.shape[0] or c < through_ref.shape[0]:
                run_ref[c] = pair(product(run_ref[c], run_ref[earlier]))
    for c in range(through_ref.shape[0]):
        through_ref[c] = run_ref[c]


def values_kernel(width, at_ref, taps_ref, raw_ref, extra_ref, show_ref, factor_ref, value_ref, memory_ref, final_ref, ext_ref):
    chunks, span, depth = raw_ref.shape[0], raw_ref.shape[1] // 2, raw_ref.shape[2]
    taps = head_taps(at_ref, taps_ref, depth)[2 * (width + 1) : 3 * (width + 1)]
    states = []
    for c in range(chunks):
        extra = extra_ref[c].astype(F32)
        value = pair(activated(raw_ref[c, :span, :], extra[2 * width : 3 * width], taps, ext_ref.at[c]))
        value_ref[c] = value
        states.append(product(show_ref[c], value))
    at = 0
    for level in scan_plan(chunks):
        for c, earlier in level:
            states[c] = states[c] + product(factor_ref[at], pair(states[earlier]))
            at += 1
    for c in range(chunks):
        memory_ref[c] = pair(states[c])
    final_ref[...] = states[chunks - 1]


def queries_kernel(width, at_ref, taps_ref, raw_ref, extra_ref, key_ref, mix_ref, value_ref, through_ref, memory_ref, local_ref, carry_ref, ext_ref):
    chunks, span, depth = raw_ref.shape[0], raw_ref.shape[1] // 2, raw_ref.shape[2]
    row, col, _ = grids(span)
    taps = head_taps(at_ref, taps_ref, depth)[: width + 1]
    for c in range(chunks):
        extra = extra_ref[c].astype(F32)
        query = unit(activated(raw_ref[c, span:, :], extra[:width], taps, ext_ref.at[c]))
        scores = jnp.where(row >= col, product_t(pair(query), key_ref[c]), 0.0)
        mixed = pair(product(pair(scores), mix_ref[c]))
        seen = pair(query - product(mixed, key_ref[c]))
        local = product(mixed, value_ref[c])
        if c == 0:
            local_ref[c] = local
            carry_ref[c] = seen
        else:
            local_ref[c] = local + product(seen, memory_ref[c - 1])
            carry_ref[c] = pair(product(seen, through_ref[c - 1]))


def finish_kernel(at_ref, local_ref, carry_ref, memory_ref, gain_ref, out_ref):
    memory = pair(jnp.where(at_ref[1] > 0, memory_ref[...], 0.0))
    gain = gain_ref[...]
    for c in range(local_ref.shape[0]):
        output = local_ref[c] + product(carry_ref[c], memory)
        scale = lax.rsqrt(jnp.mean(output * output, axis=-1, keepdims=True) + 1e-05)
        out_ref[c] = (output * scale * gain).astype(BF16)


def unpack_kernel(piece_ref, out_ref):
    depth = piece_ref.shape[2]
    for head in range(piece_ref.shape[0]):
        out_ref[:, head * depth : (head + 1) * depth] = piece_ref[head]


def compose(later, earlier):
    join = functools.partial(jnp.einsum, "ij,jk->ik", precision=lax.Precision.HIGHEST)
    return jnp.stack([join(later[0], earlier[0]), join(later[0], earlier[1]) + later[1]])


WHOLE = pl.BlockSpec(memory_space=pltpu.VMEM)
SCALAR = pl.BlockSpec(memory_space=pltpu.SMEM)
ANY = pl.BlockSpec(memory_space=pl.ANY)


def call(kernel, name, specs, args, outs, scratch=(), limit=VMEM_LIMIT):
    shapes = [jax.ShapeDtypeStruct(shape, dtype) for shape, dtype in outs]
    single = len(shapes) == 1
    return pl.pallas_call(
        kernel,
        out_shape=shapes[0] if single else shapes,
        in_specs=specs,
        out_specs=WHOLE if single else [WHOLE] * len(shapes),
        scratch_shapes=scratch,
        compiler_params=pltpu.CompilerParams(vmem_limit_bytes=limit),
        name=name,
    )(*args)


def shards(queries, key_rows, value_rows, strength, conv_weight, out_gain):
    taps = conv_weight.shape[1]
    width = taps - 1
    span, heads = strength.shape
    depth = queries.shape[1] // heads
    count = lax.axis_size("seq")
    place = lax.axis_index("seq")
    blocks = count // heads
    assert blocks * heads == count and span == depth
    groups = [[b * heads + h for h in range(heads)] for b in range(blocks)]
    block, head = place // heads, place % heads
    at = jnp.stack([head, block]).astype(jnp.int32)

    def share(x):
        return lax.all_to_all(x, "seq", 0, 0, axis_index_groups=groups, tiled=True)

    rows = pltpu.VMEM((span, heads * depth), BF16)
    tile = ((EXTRA, heads * depth), BF16)
    others, tail, rates = call(
        functools.partial(pack_kernel, width),
        "pack",
        [ANY] * 3 + [WHOLE],
        (queries, key_rows, value_rows, strength.T),
        [((heads, 2 * span, depth), BF16), tile, tile],
        [rows, pltpu.VMEM(*tile), rows]
        + [pltpu.VMEM((3, heads, span), F32), pltpu.VMEM(tile[0], F32), pltpu.SemaphoreType.DMA((3,))],
        limit=VMEM_ALL,
    )
    tail = lax.ppermute(tail, "seq", [(i, i + 1) for i in range(count - 1)])
    keys = call(
        halo_kernel,
        "halo",
        [WHOLE] * 3,
        (tail, rates, key_rows),
        [((heads, span + EXTRA, depth), BF16)],
    )
    keys = share(keys)
    others = share(others)
    taps_flat = conv_weight.reshape(3 * taps, heads * depth)
    ext = [pltpu.VMEM((heads, span + 8, depth), F32)]
    pairs = ((heads, span, 2 * depth), BF16)
    key, mix, show, extra, factor, through = call(
        functools.partial(keys_kernel, width),
        "keys",
        [SCALAR] + [WHOLE] * 2,
        (at, taps_flat, keys),
        [pairs] * 3
        + [((heads, EXTRA, depth), BF16)]
        + [((sum(map(len, scan_plan(heads))), depth, 2 * depth), BF16)]
        + [((heads - (blocks <= 2), depth, 2 * depth), BF16)],
        ext + [pltpu.VMEM((heads, depth, 2 * depth), BF16)],
    )
    value, memories, final = call(
        functools.partial(values_kernel, width),
        "values",
        [SCALAR] + [WHOLE] * 5,
        (at, taps_flat, others, extra, show, factor),
        [pairs, ((heads, depth, 2 * depth), BF16), ((depth, depth), F32)],
        ext,
    )
    ring = [(i, (i + heads) % count) for i in range(count)]
    if blocks <= 2:
        memory = lax.ppermute(final, "seq", ring)
    else:
        start = jnp.stack([jnp.eye(depth, dtype=F32), jnp.zeros((depth, depth), F32)])
        whole = through[-1, :, :depth].astype(F32) + through[-1, :, depth:].astype(F32)
        arrived = lax.ppermute(jnp.stack([whole, final]), "seq", ring)
        prefix = jnp.where(block > 0, arrived, start)
        reach = 1
        while reach < blocks - 1:
            shift = [(i, (i + reach * heads) % count) for i in range(count)]
            arrived = lax.ppermute(prefix, "seq", shift)
            prefix = jnp.where(block >= reach, compose(prefix, arrived), prefix)
            reach *= 2
        memory = prefix[1]
    local, carry = call(
        functools.partial(queries_kernel, width),
        "queries",
        [SCALAR] + [WHOLE] * 8,
        (at, taps_flat, others, extra, key, mix, value, through, memories),
        [((heads, span, depth), F32), pairs],
        ext,
    )
    mixed = call(
        finish_kernel,
        "finish",
        [SCALAR] + [WHOLE] * 4,
        (at, local, carry, memory, out_gain.reshape(1, depth)),
        [((heads, span, depth), BF16)],
    )
    return call(unpack_kernel, "unpack", [WHOLE], (share(mixed),), [((span, heads * depth), BF16)])


def solution(mesh):
    placed = (
        P(("groups", "seq"), None),
        P(("groups", "seq"), None),
        P(("groups", "seq"), None),
        P(("groups", "seq"), None),
        P(),
        P(),
    )
    return jax.shard_map(
        shards, mesh=mesh, in_specs=placed, out_specs=P(("groups", "seq"), None), check_vma=False
    )
```

```python
import functools

import jax
import jax.numpy as jnp
from jax import lax
from jax.experimental import pallas as pl
from jax.experimental.pallas import tpu as pltpu
from jax.sharding import PartitionSpec as P

EXTRA = 16
VMEM_LIMIT = 24 * 1024 * 1024
VMEM_PACK = 66200000
F32 = jnp.float32
BF16 = jnp.bfloat16


def pair(x):
    high = x.astype(BF16)
    return jnp.concatenate([high, (x - high.astype(F32)).astype(BF16)], axis=1)


def product(lhs, rhs):
    both = jnp.dot(lhs, jnp.concatenate([rhs, rhs], axis=0), preferred_element_type=F32)
    half = both.shape[1] // 2
    return both[:, :half] + both[:, half:]


def product_t(lhs, rhs):
    k = rhs.shape[1] // 2
    high, low = rhs[:, :k], rhs[:, k:]
    rhs = jnp.concatenate(
        [jnp.concatenate([high, high], axis=1), jnp.concatenate([low, low], axis=1)], axis=0
    )
    both = lax.dot_general(lhs, rhs, (((1,), (1,)), ((), ())), preferred_element_type=F32)
    half = both.shape[1] // 2
    return both[:, :half] + both[:, half:]


def pack_kernel(q_hbm, k_hbm, v_hbm, rate_ref, out_ref, q_ref, k_ref, v_ref, parts_ref, sems):
    heads, span = rate_ref.shape
    depth = q_ref.shape[1] // heads
    staged = (q_ref, k_ref, v_ref)
    copies = [
        pltpu.make_async_copy(source, target, sems.at[index])
        for index, (source, target) in enumerate(zip((q_hbm, k_hbm, v_hbm), staged))
    ]
    for copy in copies:
        copy.start()
    rate = rate_ref[...]
    parts_ref[...] = jnp.zeros_like(parts_ref)
    for part in range(3):
        high = rate.astype(BF16).astype(F32)
        for head in range(heads):
            parts_ref[head, part : part + 1, :] = high[head : head + 1]
        rate = rate - high
    for head in range(heads):
        out_ref[head, 3 * span :, :] = parts_ref[head].astype(BF16)
    for index, source in enumerate(staged):
        copies[index].wait()
        for head in range(heads):
            rows = slice(index * span, (index + 1) * span)
            out_ref[head, rows, :] = source[:, head * depth : (head + 1) * depth]


def head_taps(at_ref, taps_ref, depth):
    return taps_ref[:, pl.ds(pl.multiple_of(at_ref[0] * depth, depth), depth)].astype(F32)


def convolved(ext_ref, first, rows, taps):
    total = ext_ref[first : first + rows, :] * taps[:1]
    for tap in range(1, taps.shape[0]):
        total += ext_ref[first + tap : first + tap + rows, :] * taps[tap : tap + 1]
    return total / (1.0 + jnp.exp(-total))


def stage(raw_ref, index, ext_ref):
    span = (raw_ref.shape[1] - EXTRA) // 3
    ext_ref[:8, :] = jnp.zeros_like(ext_ref[:8, :])
    for c in range(raw_ref.shape[0]):
        rows = raw_ref[c, index * span : (index + 1) * span, :]
        ext_ref[8 + c * span : 8 + (c + 1) * span, :] = rows.astype(F32)


def taken(index, taps, width):
    return taps[index * (width + 1) : (index + 1) * (width + 1)]


def rate_row(raw_ref, c):
    span = (raw_ref.shape[1] - EXTRA) // 3
    parts = raw_ref[c, 3 * span :, :].astype(F32)
    return parts[:1] + parts[1:2] + parts[2:3]


def unit(x):
    return x * lax.rsqrt(jnp.sum(x * x, axis=-1, keepdims=True) + 1e-06)


def grids(span):
    row = lax.broadcasted_iota(jnp.int32, (span, span), 0)
    col = lax.broadcasted_iota(jnp.int32, (span, span), 1)
    return row, col, (row == col).astype(F32)


def scan_plan(chunks):
    plan, reach = [], 1
    while reach < chunks:
        plan.append([(c, (c // reach) * reach - 1) for c in range(chunks) if c // reach % 2])
        reach *= 2
    return plan


def keys_kernel(width, at_ref, taps_ref, raw_ref, key_ref, mix_ref, show_ref, factor_ref, through_ref, ext_ref, run_ref):
    chunks, depth = raw_ref.shape[0], raw_ref.shape[2]
    span = (raw_ref.shape[1] - EXTRA) // 3
    row, col, eye = grids(span)
    taps = taken(1, head_taps(at_ref, taps_ref, depth), width)
    stage(raw_ref, 1, ext_ref)
    lowers, inverses, rates, turned = [], [], [], []
    for c in range(chunks):
        key = unit(convolved(ext_ref, 8 - width + c * span, span, taps))
        rates.append(rate_row(raw_ref, c))
        if c == 0:
            rates[c] = jnp.where((col[:1] < width) & (at_ref[1] > 0), 0.0, rates[c])
        rate = jnp.sum(eye * rates[c], axis=1, keepdims=True)
        key_pair = pair(key)
        key_ref[c] = key_pair
        turned.append(pair(key.T))
        lowers.append(jnp.where(row > col, rate * product_t(key_pair, key_pair), 0.0))
        inverses.append(eye - jnp.where((row ^ col) == 1, lowers[c], 0.0))
    size = 2
    while size < span:
        pick = ((row ^ col) < 2 * size) & ((row & size) != (col & size))
        for c in range(chunks):
            inverse = pair(inverses[c])
            inner = product(pair(jnp.where(pick, lowers[c], 0.0)), inverse)
            inverses[c] = inverses[c] - product(inverse, pair(inner))
        size *= 2
    for c in range(chunks):
        mix = pair(inverses[c] * rates[c])
        mix_ref[c] = mix
        show = pair(product(turned[c], mix))
        show_ref[c] = show
        run_ref[c] = pair(eye - product(show, key_ref[c]))
    at = 0
    for level in scan_plan(chunks):
        for c, earlier in level:
            factor_ref[at] = run_ref[c]
            at += 1
            if at < factor_ref.shape[0] or c < through_ref.shape[0]:
                run_ref[c] = pair(product(run_ref[c], run_ref[earlier]))
    for c in range(through_ref.shape[0]):
        through_ref[c] = run_ref[c]


def values_kernel(width, at_ref, taps_ref, raw_ref, show_ref, factor_ref, value_ref, memory_ref, final_ref, ext_ref):
    chunks, depth = raw_ref.shape[0], raw_ref.shape[2]
    span = (raw_ref.shape[1] - EXTRA) // 3
    taps = taken(2, head_taps(at_ref, taps_ref, depth), width)
    stage(raw_ref, 2, ext_ref)
    states = []
    for c in range(chunks):
        value = pair(convolved(ext_ref, 8 - width + c * span, span, taps))
        value_ref[c] = value
        states.append(product(show_ref[c], value))
    at = 0
    for level in scan_plan(chunks):
        for c, earlier in level:
            states[c] = states[c] + product(factor_ref[at], pair(states[earlier]))
            at += 1
    for c in range(chunks - 1):
        memory_ref[c] = pair(states[c])
    final_ref[:depth, :] = states[chunks - 1]
    for index in range(3):
        tail = raw_ref[chunks - 1, (index + 1) * span - 8 : (index + 1) * span, :]
        final_ref[depth + 8 * index : depth + 8 * index + 8, :] = tail.astype(F32)


def queries_kernel(width, at_ref, taps_ref, raw_ref, key_ref, mix_ref, value_ref, through_ref, memory_ref, local_ref, carry_ref, ext_ref):
    chunks, depth = raw_ref.shape[0], raw_ref.shape[2]
    span = (raw_ref.shape[1] - EXTRA) // 3
    row, col, _ = grids(span)
    taps = taken(0, head_taps(at_ref, taps_ref, depth), width)
    stage(raw_ref, 0, ext_ref)
    for c in range(chunks):
        query = unit(convolved(ext_ref, 8 - width + c * span, span, taps))
        scores = jnp.where(row >= col, product_t(pair(query), key_ref[c]), 0.0)
        mixed = pair(product(pair(scores), mix_ref[c]))
        seen = pair(query - product(mixed, key_ref[c]))
        local = product(mixed, value_ref[c])
        if c == 0:
            local_ref[c] = local
            carry_ref[c] = seen
        else:
            local_ref[c] = local + product(seen, memory_ref[c - 1])
            carry_ref[c] = pair(product(seen, through_ref[c - 1]))


def opening(width, taps, tails, heads_of, rates, ext_ref):
    made = []
    for index in range(3):
        ext_ref[index, :8, :] = tails[8 * index : 8 * index + 8]
        ext_ref[index, 8:, :] = heads_of[index]
        made.append(convolved(ext_ref.at[index], 8 - width, 8, taken(index, taps, width)))
    row = lax.broadcasted_iota(jnp.int32, (8, rates.shape[1]), 0)
    col = lax.broadcasted_iota(jnp.int32, (8, rates.shape[1]), 1)
    strengths = jnp.sum(jnp.where((row == col) & (row < width), rates, 0.0), axis=1, keepdims=True)
    return unit(made[0]), unit(made[1]), made[2], strengths


def first_rows(raw_ref):
    span = (raw_ref.shape[1] - EXTRA) // 3
    return [raw_ref[0, index * span : index * span + 16, :].astype(F32)[:8] for index in range(3)]


def finish_kernel(width, at_ref, taps_ref, raw_ref, local_ref, carry_ref, memory_ref, gain_ref, out_ref, ext_ref, first_ref):
    depth = local_ref.shape[2]
    later = at_ref[1] > 0
    memory = jnp.where(later, memory_ref[:depth, :], 0.0)
    tails = memory_ref[depth:, :]
    taps = head_taps(at_ref, taps_ref, depth)
    query, key, value, rate = opening(width, taps, tails, first_rows(raw_ref), rate_row(raw_ref, 0), ext_ref)
    rate = jnp.where(later, rate, 0.0)
    seen = product(pair(jnp.concatenate([key, query], axis=0)), pair(memory))
    delta = rate * (value - seen[:8])
    row = lax.broadcasted_iota(jnp.int32, delta.shape, 0)
    output = seen[8:]
    for t in range(width):
        now = delta[t : t + 1]
        meets = jnp.sum(key * key[t : t + 1], axis=1, keepdims=True)
        delta = jnp.where(row > t, delta - rate * meets * now, delta)
        shown = jnp.sum(query * key[t : t + 1], axis=1, keepdims=True)
        output = jnp.where(row >= t, output + shown * now, output)
    delta = jnp.where(row < width, delta, 0.0)
    turn = (((0,), (0,)), ((), ()))
    key_pair, delta_pair = pair(key), pair(delta)
    both = lax.dot_general(key_pair, delta_pair, turn, preferred_element_type=F32)
    both = both[:depth] + both[depth:]
    memory = pair(memory + both[:, :depth] + both[:, depth:])
    first_ref[...] = output
    gain = gain_ref[...]
    for c in range(local_ref.shape[0]):
        output = local_ref[c] + product(carry_ref[c], memory)
        if c == 0:
            tall = lax.broadcasted_iota(jnp.int32, output.shape, 0)
            opened = jnp.concatenate([first_ref[...]] + [jnp.zeros_like(output[8:])], axis=0)
            output = jnp.where((tall < width) & later, opened, output)
        scale = lax.rsqrt(jnp.mean(output * output, axis=-1, keepdims=True) + 1e-05)
        out_ref[c] = (output * scale * gain).astype(BF16)


def unpack_kernel(piece_ref, out_ref):
    depth = piece_ref.shape[2]
    for head in range(piece_ref.shape[0]):
        out_ref[:, head * depth : (head + 1) * depth] = piece_ref[head]


def compose(later, earlier):
    join = functools.partial(jnp.einsum, "ij,jk->ik", precision=lax.Precision.HIGHEST)
    return jnp.stack([join(later[0], earlier[0]), join(later[0], earlier[1]) + later[1]])


def opening_map(width, taps, tails, raw):
    span = (raw.shape[1] - EXTRA) // 3
    made = []
    for index in range(1, 3):
        rows = jnp.concatenate(
            [tails[8 * index + 8 - width : 8 * index + 8], raw[0, index * span : index * span + width].astype(F32)]
        )
        own = taken(index, taps, width)
        total = sum(rows[tap : tap + width] * own[tap] for tap in range(width + 1))
        made.append(total / (1.0 + jnp.exp(-total)))
    keys = unit(made[0])
    rates = jnp.sum(raw[0, 3 * span : 3 * span + 3].astype(F32), axis=0)
    depth = keys.shape[1]
    maps = jnp.stack([jnp.eye(depth, dtype=F32), jnp.zeros((depth, depth), F32)])
    for t in range(width):
        outer = rates[t] * keys[t][:, None]
        one = jnp.stack([jnp.eye(depth, dtype=F32) - outer * keys[t], outer * made[1][t]])
        maps = compose(one, maps)
    return maps


WHOLE = pl.BlockSpec(memory_space=pltpu.VMEM)
SCALAR = pl.BlockSpec(memory_space=pltpu.SMEM)
ANY = pl.BlockSpec(memory_space=pl.ANY)


def call(kernel, name, specs, args, outs, scratch=(), limit=VMEM_LIMIT):
    shapes = [jax.ShapeDtypeStruct(shape, dtype) for shape, dtype in outs]
    single = len(shapes) == 1
    return pl.pallas_call(
        kernel,
        out_shape=shapes[0] if single else shapes,
        in_specs=specs,
        out_specs=WHOLE if single else [WHOLE] * len(shapes),
        scratch_shapes=scratch,
        compiler_params=pltpu.CompilerParams(vmem_limit_bytes=limit),
        name=name,
    )(*args)


def shards(queries, key_rows, value_rows, strength, conv_weight, out_gain):
    taps = conv_weight.shape[1]
    width = taps - 1
    span, heads = strength.shape
    depth = queries.shape[1] // heads
    count = lax.axis_size("seq")
    place = lax.axis_index("seq")
    blocks = count // heads
    assert blocks * heads == count and span == depth
    groups = [[b * heads + h for h in range(heads)] for b in range(blocks)]
    block, head = place // heads, place % heads
    at = jnp.stack([head, block]).astype(jnp.int32)

    def share(x):
        return lax.all_to_all(x, "seq", 0, 0, axis_index_groups=groups, tiled=True)

    rows = pltpu.VMEM((span, heads * depth), BF16)
    raw = call(
        pack_kernel,
        "pack",
        [ANY] * 3 + [WHOLE],
        (queries, key_rows, value_rows, strength.T),
        [((heads, 3 * span + EXTRA, depth), BF16)],
        [rows] * 3 + [pltpu.VMEM((heads, EXTRA, depth), F32), pltpu.SemaphoreType.DMA((3,))],
        limit=VMEM_PACK,
    )
    raw = share(raw)
    taps_flat = conv_weight.reshape(3 * taps, heads * depth)
    ext = [pltpu.VMEM((heads * span + 8, depth), F32)]
    pairs = ((heads, span, 2 * depth), BF16)
    square = (depth, 2 * depth)
    key, mix, show, factor, through = call(
        functools.partial(keys_kernel, width),
        "keys",
        [SCALAR] + [WHOLE] * 2,
        (at, taps_flat, raw),
        [pairs] * 3
        + [((sum(map(len, scan_plan(heads))), *square), BF16)]
        + [((heads - (blocks <= 2), *square), BF16)],
        ext + [pltpu.VMEM((heads, *square), BF16)],
    )
    value, memories, final = call(
        functools.partial(values_kernel, width),
        "values",
        [SCALAR] + [WHOLE] * 4,
        (at, taps_flat, raw, show, factor),
        [pairs, ((heads - 1, *square), BF16), ((depth + 24, depth), F32)],
        ext,
    )
    ring = [(i, (i + heads) % count) for i in range(count)]
    memory = lax.ppermute(final, "seq", ring)
    if blocks > 2:
        tails = memory[depth:]
        start = jnp.stack([jnp.eye(depth, dtype=F32), jnp.zeros((depth, depth), F32)])
        whole = through[-1, :, :depth].astype(F32) + through[-1, :, depth:].astype(F32)
        own = lax.dynamic_slice_in_dim(taps_flat, head * depth, depth, 1).astype(F32)
        opened = jnp.where(block > 0, opening_map(width, own, tails, raw), start)
        arrived = lax.ppermute(compose(jnp.stack([whole, final[:depth]]), opened), "seq", ring)
        prefix = jnp.where(block > 0, arrived, start)
        reach = 1
        while reach < blocks - 1:
            shift = [(i, (i + reach * heads) % count) for i in range(count)]
            arrived = lax.ppermute(prefix, "seq", shift)
            prefix = jnp.where(block >= reach, compose(prefix, arrived), prefix)
            reach *= 2
        memory = jnp.concatenate([prefix[1], tails])
    local, carry = call(
        functools.partial(queries_kernel, width),
        "queries",
        [SCALAR] + [WHOLE] * 7,
        (at, taps_flat, raw, key, mix, value, through, memories),
        [((heads, span, depth), F32), pairs],
        ext,
    )
    mixed = call(
        functools.partial(finish_kernel, width),
        "finish",
        [SCALAR] + [WHOLE] * 6,
        (at, taps_flat, raw, local, carry, memory, out_gain.reshape(1, depth)),
        [((heads, span, depth), BF16)],
        [pltpu.VMEM((3, 16, depth), F32), pltpu.VMEM((8, depth), F32)],
    )
    return call(unpack_kernel, "unpack", [WHOLE], (share(mixed),), [((span, heads * depth), BF16)])


def solution(mesh):
    placed = (
        P(("groups", "seq"), None),
        P(("groups", "seq"), None),
        P(("groups", "seq"), None),
        P(("groups", "seq"), None),
        P(),
        P(),
    )
    return jax.shard_map(
        shards, mesh=mesh, in_specs=placed, out_specs=P(("groups", "seq"), None), check_vma=False
    )
```

```python
import functools

import jax
import jax.numpy as jnp
from jax import lax
from jax.experimental import pallas as pl
from jax.experimental.pallas import tpu as pltpu
from jax.sharding import PartitionSpec as P

EXTRA = 8
VMEM_LIMIT = 24 * 1024 * 1024
VMEM_PACK = 66200000
F32 = jnp.float32
BF16 = jnp.bfloat16


def pair(x):
    high = x.astype(BF16)
    return jnp.concatenate([high, (x - high.astype(F32)).astype(BF16)], axis=1)


def product(lhs, rhs):
    both = jnp.dot(lhs, jnp.concatenate([rhs, rhs], axis=0), preferred_element_type=F32)
    half = both.shape[1] // 2
    return both[:, :half] + both[:, half:]


def product_t(lhs, rhs):
    k = rhs.shape[1] // 2
    high, low = rhs[:, :k], rhs[:, k:]
    rhs = jnp.concatenate(
        [jnp.concatenate([high, high], axis=1), jnp.concatenate([low, low], axis=1)], axis=0
    )
    both = lax.dot_general(lhs, rhs, (((1,), (1,)), ((), ())), preferred_element_type=F32)
    half = both.shape[1] // 2
    return both[:, :half] + both[:, half:]


def pack_kernel(at_ref, q_hbm, k_hbm, v_hbm, rate_ref, keys_ref, *refs):
    pieces, (q_ref, k_ref, v_ref, parts_ref, sems) = refs[:-5], refs[-5:]
    heads, span = rate_ref.shape
    depth = q_ref.shape[1] // heads
    copies = [
        pltpu.make_async_copy(source, target, sems.at[index])
        for index, (source, target) in enumerate(((k_hbm, k_ref), (v_hbm, v_ref), (q_hbm, q_ref)))
    ]
    for copy in copies:
        copy.start()
    rate = rate_ref[...]
    parts_ref[...] = jnp.zeros_like(parts_ref)
    for part in range(3):
        high = rate.astype(BF16).astype(F32)
        for head in range(heads):
            parts_ref[head, part : part + 1, :] = high[head : head + 1]
        rate = rate - high
    for head in range(heads):
        keys_ref[head, span:, :] = parts_ref[head].astype(BF16)
    copies[0].wait()
    for head in range(heads):
        keys_ref[head, :span, :] = k_ref[:, head * depth : (head + 1) * depth]
    for index, source in enumerate((v_ref, q_ref)):
        copies[1 + index].wait()
        for slot in range(heads):
            lanes = pl.ds(pl.multiple_of((at_ref[0] ^ slot) * depth, depth), depth)
            pieces[slot][index * span : (index + 1) * span, :] = source[:, lanes]


def head_taps(at_ref, taps_ref, depth):
    return taps_ref[:, pl.ds(pl.multiple_of(at_ref[0] * depth, depth), depth)].astype(F32)


def convolved(ext_ref, first, rows, taps):
    total = ext_ref[first : first + rows, :] * taps[:1]
    for tap in range(1, taps.shape[0]):
        total += ext_ref[first + tap : first + tap + rows, :] * taps[tap : tap + 1]
    return total / (1.0 + jnp.exp(-total))


def stage_keys(raw_ref, ext_ref):
    span = raw_ref.shape[1] - EXTRA
    ext_ref[:8, :] = jnp.zeros_like(ext_ref[:8, :])
    for c in range(raw_ref.shape[0]):
        ext_ref[8 + c * span : 8 + (c + 1) * span, :] = raw_ref[c, :span, :].astype(F32)


def stage(at_ref, pieces, index, ext_ref):
    span = pieces[0].shape[0] // 2
    ext_ref[:8, :] = jnp.zeros_like(ext_ref[:8, :])
    for slot, piece in enumerate(pieces):
        rows = pl.ds(pl.multiple_of(8 + (at_ref[0] ^ slot) * span, 8), span)
        ext_ref[rows, :] = piece[index * span : (index + 1) * span, :].astype(F32)


def taken(index, taps, width):
    return taps[index * (width + 1) : (index + 1) * (width + 1)]


def rate_row(raw_ref, c):
    parts = raw_ref[c, raw_ref.shape[1] - EXTRA :, :].astype(F32)
    return parts[:1] + parts[1:2] + parts[2:3]


def unit(x):
    return x * lax.rsqrt(jnp.sum(x * x, axis=-1, keepdims=True) + 1e-06)


def grids(span):
    row = lax.broadcasted_iota(jnp.int32, (span, span), 0)
    col = lax.broadcasted_iota(jnp.int32, (span, span), 1)
    return row, col, (row == col).astype(F32)


def scan_plan(chunks):
    plan, reach = [], 1
    while reach < chunks:
        plan.append([(c, (c // reach) * reach - 1) for c in range(chunks) if c // reach % 2])
        reach *= 2
    return plan


def keys_kernel(width, at_ref, taps_ref, gain_ref, raw_ref, gain_out, key_ref, mix_ref, show_ref, factor_ref, through_ref, ext_ref, run_ref):
    gain_out[...] = gain_ref[...]
    chunks, depth = raw_ref.shape[0], raw_ref.shape[2]
    span = raw_ref.shape[1] - EXTRA
    row, col, eye = grids(span)
    taps = taken(1, head_taps(at_ref, taps_ref, depth), width)
    stage_keys(raw_ref, ext_ref)
    lowers, inverses, rates, turned = [], [], [], []
    for c in range(chunks):
        key = unit(convolved(ext_ref, 8 - width + c * span, span, taps))
        rates.append(rate_row(raw_ref, c))
        if c == 0:
            rates[c] = jnp.where((col[:1] < width) & (at_ref[1] > 0), 0.0, rates[c])
        rate = jnp.sum(eye * rates[c], axis=1, keepdims=True)
        key_pair = pair(key)
        key_ref[c] = key_pair
        turned.append(pair(key.T))
        lowers.append(jnp.where(row > col, rate * product_t(key_pair, key_pair), 0.0))
        inverses.append(eye - jnp.where((row ^ col) == 1, lowers[c], 0.0))
    size = 2
    while size < span:
        pick = ((row ^ col) < 2 * size) & ((row & size) != (col & size))
        for c in range(chunks):
            inverse = pair(inverses[c])
            inner = product(pair(jnp.where(pick, lowers[c], 0.0)), inverse)
            inverses[c] = inverses[c] - product(inverse, pair(inner))
        size *= 2
    for c in range(chunks):
        mix = pair(inverses[c] * rates[c])
        mix_ref[c] = mix
        show = pair(product(turned[c], mix))
        show_ref[c] = show
        run_ref[c] = pair(eye - product(show, key_ref[c]))
    at = 0
    for level in scan_plan(chunks):
        for c, earlier in level:
            factor_ref[at] = run_ref[c]
            at += 1
            if at < factor_ref.shape[0] or c < through_ref.shape[0]:
                run_ref[c] = pair(product(run_ref[c], run_ref[earlier]))
    for c in range(through_ref.shape[0]):
        through_ref[c] = run_ref[c]


def values_kernel(width, at_ref, taps_ref, raw_ref, show_ref, factor_ref, *refs):
    pieces, (value_ref, memory_ref, final_ref, first_ref, ext_ref, edge_ref) = refs[:-6], refs[-6:]
    chunks, depth = raw_ref.shape[0], raw_ref.shape[2]
    span = raw_ref.shape[1] - EXTRA
    taps = taken(2, head_taps(at_ref, taps_ref, depth), width)
    stage(at_ref, pieces, 0, ext_ref)
    states = []
    for c in range(chunks):
        value = pair(convolved(ext_ref, 8 - width + c * span, span, taps))
        value_ref[c] = value
        states.append(product(show_ref[c], value))
    at = 0
    for level in scan_plan(chunks):
        for c, earlier in level:
            states[c] = states[c] + product(factor_ref[at], pair(states[earlier]))
            at += 1
    for c in range(chunks - 1):
        memory_ref[c] = pair(states[c])
    final_ref[:depth, :] = states[chunks - 1]
    for slot, piece in enumerate(pieces):
        chunk = at_ref[0] ^ slot
        edge_ref[0, pl.ds(pl.multiple_of(8 * chunk, 8), 8), :] = piece[span : span + 8, :].astype(F32)
        edge_ref[1, pl.ds(pl.multiple_of(8 * chunk, 8), 8), :] = piece[2 * span - 8 :, :].astype(F32)
    last = 8 * (chunks - 1)
    final_ref[depth : depth + 8, :] = edge_ref[1, last : last + 8, :]
    final_ref[depth + 8 : depth + 16, :] = raw_ref[chunks - 1, span - 8 : span, :].astype(F32)
    final_ref[depth + 16 : depth + 24, :] = ext_ref[chunks * span : chunks * span + 8, :]
    first_ref[:8, :] = edge_ref[0, :8, :]
    first_ref[8:16, :] = raw_ref[0, :8, :].astype(F32)
    first_ref[16:24, :] = ext_ref[8:16, :]
    first_ref[24:25, :] = rate_row(raw_ref, 0)


def queries_kernel(width, at_ref, taps_ref, key_ref, mix_ref, value_ref, through_ref, memory_ref, *refs):
    pieces, (local_ref, carry_ref, ext_ref) = refs[:-3], refs[-3:]
    chunks, span, depth = key_ref.shape[0], key_ref.shape[1], key_ref.shape[2] // 2
    row, col, _ = grids(span)
    taps = taken(0, head_taps(at_ref, taps_ref, depth), width)
    stage(at_ref, pieces, 1, ext_ref)
    queries = [unit(convolved(ext_ref, 8 - width + c * span, span, taps)) for c in range(chunks)]
    mixed = [
        pair(jnp.where(row >= col, product_t(pair(queries[c]), key_ref[c]), 0.0)) for c in range(chunks)
    ]
    mixed = [pair(product(mixed[c], mix_ref[c])) for c in range(chunks)]
    seen = [pair(queries[c] - product(mixed[c], key_ref[c])) for c in range(chunks)]
    local = [product(mixed[c], value_ref[c]) for c in range(chunks)]
    local_ref[0] = local[0]
    carry_ref[0] = seen[0]
    for c in range(1, chunks):
        local_ref[c] = local[c] + product(seen[c], memory_ref[c - 1])
        carry_ref[c] = pair(product(seen[c], through_ref[c - 1]))


def opening(width, taps, tails, start_ref, ext_ref):
    made = []
    for index in range(3):
        ext_ref[index, :8, :] = tails[8 * index : 8 * index + 8]
        ext_ref[index, 8:, :] = start_ref[8 * index : 8 * index + 8, :]
        made.append(convolved(ext_ref.at[index], 8 - width, 8, taken(index, taps, width)))
    rates = start_ref[24:25, :]
    row = lax.broadcasted_iota(jnp.int32, (8, rates.shape[1]), 0)
    col = lax.broadcasted_iota(jnp.int32, (8, rates.shape[1]), 1)
    strengths = jnp.sum(jnp.where((row == col) & (row < width), rates, 0.0), axis=1, keepdims=True)
    return unit(made[0]), unit(made[1]), made[2], strengths


def finish_kernel(width, at_ref, taps_ref, start_ref, local_ref, carry_ref, memory_ref, gain_ref, out_ref, ext_ref, first_ref):
    depth = local_ref.shape[2]
    later = at_ref[1] > 0
    memory = jnp.where(later, memory_ref[:depth, :], 0.0)
    tails = memory_ref[depth:, :]
    taps = head_taps(at_ref, taps_ref, depth)
    query, key, value, rate = opening(width, taps, tails, start_ref, ext_ref)
    rate = jnp.where(later, rate, 0.0)
    seen = product(pair(jnp.concatenate([key, query], axis=0)), pair(memory))
    delta = rate * (value - seen[:8])
    row = lax.broadcasted_iota(jnp.int32, delta.shape, 0)
    output = seen[8:]
    for t in range(width):
        now = delta[t : t + 1]
        meets = jnp.sum(key * key[t : t + 1], axis=1, keepdims=True)
        delta = jnp.where(row > t, delta - rate * meets * now, delta)
        shown = jnp.sum(query * key[t : t + 1], axis=1, keepdims=True)
        output = jnp.where(row >= t, output + shown * now, output)
    delta = jnp.where(row < width, delta, 0.0)
    turn = (((0,), (0,)), ((), ()))
    key_pair, delta_pair = pair(key), pair(delta)
    both = lax.dot_general(key_pair, delta_pair, turn, preferred_element_type=F32)
    both = both[:depth] + both[depth:]
    memory = pair(memory + both[:, :depth] + both[:, depth:])
    first_ref[...] = output
    gain = gain_ref[...]
    for c in range(local_ref.shape[0]):
        output = local_ref[c] + product(carry_ref[c], memory)
        if c == 0:
            tall = lax.broadcasted_iota(jnp.int32, output.shape, 0)
            opened = jnp.concatenate([first_ref[...]] + [jnp.zeros_like(output[8:])], axis=0)
            output = jnp.where((tall < width) & later, opened, output)
        scale = lax.rsqrt(jnp.mean(output * output, axis=-1, keepdims=True) + 1e-05)
        out_ref[c] = (output * scale * gain).astype(BF16)


def unpack_kernel(piece_ref, out_ref):
    depth = piece_ref.shape[2]
    for head in range(piece_ref.shape[0]):
        out_ref[:, head * depth : (head + 1) * depth] = piece_ref[head]


def compose(later, earlier):
    join = functools.partial(jnp.einsum, "ij,jk->ik", precision=lax.Precision.HIGHEST)
    return jnp.stack([join(later[0], earlier[0]), join(later[0], earlier[1]) + later[1]])


def opening_map(width, taps, tails, first):
    made = []
    for index in range(1, 3):
        rows = jnp.concatenate(
            [tails[8 * index + 8 - width : 8 * index + 8], first[8 * index : 8 * index + width]]
        )
        own = taken(index, taps, width)
        total = sum(rows[tap : tap + width] * own[tap] for tap in range(width + 1))
        made.append(total / (1.0 + jnp.exp(-total)))
    keys = unit(made[0])
    rates = first[24]
    depth = keys.shape[1]
    maps = jnp.stack([jnp.eye(depth, dtype=F32), jnp.zeros((depth, depth), F32)])
    for t in range(width):
        outer = rates[t] * keys[t][:, None]
        one = jnp.stack([jnp.eye(depth, dtype=F32) - outer * keys[t], outer * made[1][t]])
        maps = compose(one, maps)
    return maps


WHOLE = pl.BlockSpec(memory_space=pltpu.VMEM)
SCALAR = pl.BlockSpec(memory_space=pltpu.SMEM)
ANY = pl.BlockSpec(memory_space=pl.ANY)


def call(kernel, name, specs, args, outs, scratch=(), limit=VMEM_LIMIT):
    shapes = [jax.ShapeDtypeStruct(shape, dtype) for shape, dtype in outs]
    single = len(shapes) == 1
    return pl.pallas_call(
        kernel,
        out_shape=shapes[0] if single else shapes,
        in_specs=specs,
        out_specs=WHOLE if single else [WHOLE] * len(shapes),
        scratch_shapes=scratch,
        compiler_params=pltpu.CompilerParams(vmem_limit_bytes=limit),
        name=name,
    )(*args)


def shards(queries, key_rows, value_rows, strength, conv_weight, out_gain):
    taps = conv_weight.shape[1]
    width = taps - 1
    span, heads = strength.shape
    depth = queries.shape[1] // heads
    count = lax.axis_size("seq")
    place = lax.axis_index("seq")
    blocks = count // heads
    assert blocks * heads == count and span == depth and heads & (heads - 1) == 0
    groups = [[b * heads + h for h in range(heads)] for b in range(blocks)]
    block, head = place // heads, place % heads
    at = jnp.stack([head, block]).astype(jnp.int32)

    def share(x):
        return lax.all_to_all(x, "seq", 0, 0, axis_index_groups=groups, tiled=True)

    rows = pltpu.VMEM((span, heads * depth), BF16)
    packed = call(
        pack_kernel,
        "pack",
        [SCALAR] + [ANY] * 3 + [WHOLE],
        (at, queries, key_rows, value_rows, strength.T),
        [((heads, span + EXTRA, depth), BF16)] + [((2 * span, depth), BF16)] * heads,
        [rows] * 3 + [pltpu.VMEM((heads, EXTRA, depth), F32), pltpu.SemaphoreType.DMA((3,))],
        limit=VMEM_PACK,
    )
    raw = share(packed[0])
    pieces = [packed[1]]
    for slot in range(1, heads):
        pairs = [(i, i ^ slot) for i in range(count)]
        pieces.append(lax.ppermute(packed[1 + slot], "seq", pairs))
    taps_flat = conv_weight.reshape(3 * taps, heads * depth)
    ext = [pltpu.VMEM((heads * span + 8, depth), F32)]
    pairs = ((heads, span, 2 * depth), BF16)
    square = (depth, 2 * depth)
    gain, key, mix, show, factor, through = call(
        functools.partial(keys_kernel, width),
        "keys",
        [SCALAR] + [WHOLE] * 3,
        (at, taps_flat, out_gain.reshape(1, depth), raw),
        [((1, depth), F32)]
        + [pairs] * 3
        + [((sum(map(len, scan_plan(heads))), *square), BF16)]
        + [((heads - (blocks <= 2), *square), BF16)],
        ext + [pltpu.VMEM((heads, *square), BF16)],
    )
    value, memories, final, first = call(
        functools.partial(values_kernel, width),
        "values",
        [SCALAR] + [WHOLE] * (4 + heads),
        (at, taps_flat, raw, show, factor, *pieces),
        [pairs, ((heads - 1, *square), BF16), ((depth + 24, depth), F32), ((32, depth), F32)],
        ext + [pltpu.VMEM((2, 8 * heads, depth), F32)],
    )
    ring = [(i, (i + heads) % count) for i in range(count)]
    memory = lax.ppermute(final, "seq", ring)
    if blocks > 2:
        tails = memory[depth:]
        start = jnp.stack([jnp.eye(depth, dtype=F32), jnp.zeros((depth, depth), F32)])
        whole = through[-1, :, :depth].astype(F32) + through[-1, :, depth:].astype(F32)
        own = lax.dynamic_slice_in_dim(taps_flat, head * depth, depth, 1).astype(F32)
        opened = jnp.where(block > 0, opening_map(width, own, tails, first), start)
        arrived = lax.ppermute(compose(jnp.stack([whole, final[:depth]]), opened), "seq", ring)
        prefix = jnp.where(block > 0, arrived, start)
        reach = 1
        while reach < blocks - 1:
            shift = [(i, (i + reach * heads) % count) for i in range(count)]
            arrived = lax.ppermute(prefix, "seq", shift)
            prefix = jnp.where(block >= reach, compose(prefix, arrived), prefix)
            reach *= 2
        memory = jnp.concatenate([prefix[1], tails])
    local, carry = call(
        functools.partial(queries_kernel, width),
        "queries",
        [SCALAR] + [WHOLE] * (6 + heads),
        (at, taps_flat, key, mix, value, through, memories, *pieces),
        [((heads, span, depth), F32), pairs],
        ext,
    )
    mixed = call(
        functools.partial(finish_kernel, width),
        "finish",
        [SCALAR] + [WHOLE] * 6,
        (at, taps_flat, first, local, carry, memory, gain),
        [((heads, span, depth), BF16)],
        [pltpu.VMEM((3, 16, depth), F32), pltpu.VMEM((8, depth), F32)],
    )
    return call(unpack_kernel, "unpack", [WHOLE], (share(mixed),), [((span, heads * depth), BF16)])


def solution(mesh):
    placed = (
        P(("groups", "seq"), None),
        P(("groups", "seq"), None),
        P(("groups", "seq"), None),
        P(("groups", "seq"), None),
        P(),
        P(),
    )
    return jax.shard_map(
        shards, mesh=mesh, in_specs=placed, out_specs=P(("groups", "seq"), None), check_vma=False
    )
```

```python
import functools

import jax
import jax.numpy as jnp
from jax import lax
from jax.experimental import pallas as pl
from jax.experimental.pallas import tpu as pltpu
from jax.sharding import PartitionSpec as P

EXTRA = 8
VMEM_LIMIT = 24 * 1024 * 1024
VMEM_PACK = 66200000
F32 = jnp.float32
BF16 = jnp.bfloat16


def pair(x):
    high = x.astype(BF16)
    return jnp.concatenate([high, (x - high.astype(F32)).astype(BF16)], axis=1)


def product(lhs, rhs):
    both = jnp.dot(lhs, jnp.concatenate([rhs, rhs], axis=0), preferred_element_type=F32)
    half = both.shape[1] // 2
    return both[:, :half] + both[:, half:]


def product_t(lhs, rhs):
    k = rhs.shape[1] // 2
    high, low = rhs[:, :k], rhs[:, k:]
    rhs = jnp.concatenate(
        [jnp.concatenate([high, high], axis=1), jnp.concatenate([low, low], axis=1)], axis=0
    )
    both = lax.dot_general(lhs, rhs, (((1,), (1,)), ((), ())), preferred_element_type=F32)
    half = both.shape[1] // 2
    return both[:, :half] + both[:, half:]


def pack_kernel(q_hbm, k_hbm, v_hbm, rate_ref, keys_hbm, *refs):
    pieces, (q_ref, k_ref, v_ref, parts_ref, extra_ref, in_sems, out_sems) = refs[:-7], refs[-7:]
    heads, span = rate_ref.shape
    depth = q_ref.shape[1] // heads
    own = lax.rem(lax.axis_index("seq"), heads)
    arriving = [
        pltpu.make_async_copy(source, target, in_sems.at[index])
        for index, (source, target) in enumerate(((k_hbm, k_ref), (v_hbm, v_ref), (q_hbm, q_ref)))
    ]
    for copy in arriving:
        copy.start()
    leaving = []

    def leave(source, target):
        leaving.append(pltpu.make_async_copy(source, target, out_sems.at[len(leaving)]))
        leaving[-1].start()

    rate = rate_ref[...]
    parts_ref[...] = jnp.zeros_like(parts_ref)
    for part in range(3):
        high = rate.astype(BF16).astype(F32)
        for head in range(heads):
            parts_ref[head, part : part + 1, :] = high[head : head + 1]
        rate = rate - high
    extra_ref[...] = parts_ref[...].astype(BF16)
    leave(extra_ref, keys_hbm.at[:, span:, :])
    arriving[0].wait()
    for head in range(heads):
        leave(k_ref.at[:, head * depth : (head + 1) * depth], keys_hbm.at[head, :span, :])
    for index, source in enumerate((v_ref, q_ref)):
        arriving[1 + index].wait()
        for slot in range(heads):
            lanes = pl.ds(pl.multiple_of((own ^ slot) * depth, depth), depth)
            leave(source.at[:, lanes], pieces[slot].at[index * span : (index + 1) * span, :])
    for copy in leaving:
        copy.wait()


def head_taps(at_ref, taps_ref, depth):
    return taps_ref[:, pl.ds(pl.multiple_of(at_ref[0] * depth, depth), depth)].astype(F32)


def convolved(ext_ref, first, rows, taps):
    total = ext_ref[first : first + rows, :] * taps[:1]
    for tap in range(1, taps.shape[0]):
        total += ext_ref[first + tap : first + tap + rows, :] * taps[tap : tap + 1]
    return total / (1.0 + jnp.exp(-total))


def stage_keys(raw_ref, ext_ref):
    span = raw_ref.shape[1] - EXTRA
    ext_ref[:8, :] = jnp.zeros_like(ext_ref[:8, :])
    for c in range(raw_ref.shape[0]):
        ext_ref[8 + c * span : 8 + (c + 1) * span, :] = raw_ref[c, :span, :].astype(F32)


def stage(at_ref, pieces, index, ext_ref):
    span = pieces[0].shape[0] // 2
    ext_ref[:8, :] = jnp.zeros_like(ext_ref[:8, :])
    for slot, piece in enumerate(pieces):
        rows = pl.ds(pl.multiple_of(8 + (at_ref[0] ^ slot) * span, 8), span)
        ext_ref[rows, :] = piece[index * span : (index + 1) * span, :].astype(F32)


def taken(index, taps, width):
    return taps[index * (width + 1) : (index + 1) * (width + 1)]


def rate_row(raw_ref, c):
    parts = raw_ref[c, raw_ref.shape[1] - EXTRA :, :].astype(F32)
    return parts[:1] + parts[1:2] + parts[2:3]


def unit(x):
    return x * lax.rsqrt(jnp.sum(x * x, axis=-1, keepdims=True) + 1e-06)


def grids(span):
    row = lax.broadcasted_iota(jnp.int32, (span, span), 0)
    col = lax.broadcasted_iota(jnp.int32, (span, span), 1)
    return row, col, (row == col).astype(F32)


def scan_plan(chunks):
    plan, reach = [], 1
    while reach < chunks:
        plan.append([(c, (c // reach) * reach - 1) for c in range(chunks) if c // reach % 2])
        reach *= 2
    return plan


def keys_kernel(width, at_ref, taps_ref, gain_ref, raw_ref, gain_out, key_ref, mix_ref, show_ref, factor_ref, through_ref, ext_ref, run_ref):
    gain_out[...] = gain_ref[...]
    chunks, depth = raw_ref.shape[0], raw_ref.shape[2]
    span = raw_ref.shape[1] - EXTRA
    row, col, eye = grids(span)
    taps = taken(1, head_taps(at_ref, taps_ref, depth), width)
    stage_keys(raw_ref, ext_ref)
    lowers, inverses, rates, turned = [], [], [], []
    for c in range(chunks):
        key = unit(convolved(ext_ref, 8 - width + c * span, span, taps))
        rates.append(rate_row(raw_ref, c))
        if c == 0:
            rates[c] = jnp.where((col[:1] < width) & (at_ref[1] > 0), 0.0, rates[c])
        rate = jnp.sum(eye * rates[c], axis=1, keepdims=True)
        key_pair = pair(key)
        key_ref[c] = key_pair
        turned.append(pair(key.T))
        lowers.append(jnp.where(row > col, rate * product_t(key_pair, key_pair), 0.0))
        inverses.append(eye - jnp.where((row ^ col) == 1, lowers[c], 0.0))
    size = 2
    while size < span:
        pick = ((row ^ col) < 2 * size) & ((row & size) != (col & size))
        for c in range(chunks):
            inverse = pair(inverses[c])
            inner = product(pair(jnp.where(pick, lowers[c], 0.0)), inverse)
            inverses[c] = inverses[c] - product(inverse, pair(inner))
        size *= 2
    for c in range(chunks):
        mix = pair(inverses[c] * rates[c])
        mix_ref[c] = mix
        show = pair(product(turned[c], mix))
        show_ref[c] = show
        run_ref[c] = pair(eye - product(show, key_ref[c]))
    at = 0
    for level in scan_plan(chunks):
        for c, earlier in level:
            factor_ref[at] = run_ref[c]
            at += 1
            if at < factor_ref.shape[0] or c < through_ref.shape[0]:
                run_ref[c] = pair(product(run_ref[c], run_ref[earlier]))
    for c in range(through_ref.shape[0]):
        through_ref[c] = run_ref[c]


def values_kernel(width, at_ref, taps_ref, raw_ref, show_ref, factor_ref, *refs):
    pieces, (value_ref, memory_ref, final_ref, first_ref, ext_ref, edge_ref) = refs[:-6], refs[-6:]
    chunks, depth = raw_ref.shape[0], raw_ref.shape[2]
    span = raw_ref.shape[1] - EXTRA
    taps = taken(2, head_taps(at_ref, taps_ref, depth), width)
    stage(at_ref, pieces, 0, ext_ref)
    states = []
    for c in range(chunks):
        value = pair(convolved(ext_ref, 8 - width + c * span, span, taps))
        value_ref[c] = value
        states.append(product(show_ref[c], value))
    at = 0
    for level in scan_plan(chunks):
        for c, earlier in level:
            states[c] = states[c] + product(factor_ref[at], pair(states[earlier]))
            at += 1
    for c in range(chunks - 1):
        memory_ref[c] = pair(states[c])
    final_ref[:depth, :] = states[chunks - 1]
    for slot, piece in enumerate(pieces):
        chunk = at_ref[0] ^ slot
        edge_ref[0, pl.ds(pl.multiple_of(8 * chunk, 8), 8), :] = piece[span : span + 8, :].astype(F32)
        edge_ref[1, pl.ds(pl.multiple_of(8 * chunk, 8), 8), :] = piece[2 * span - 8 :, :].astype(F32)
    last = 8 * (chunks - 1)
    final_ref[depth : depth + 8, :] = edge_ref[1, last : last + 8, :]
    final_ref[depth + 8 : depth + 16, :] = raw_ref[chunks - 1, span - 8 : span, :].astype(F32)
    final_ref[depth + 16 : depth + 24, :] = ext_ref[chunks * span : chunks * span + 8, :]
    first_ref[:8, :] = edge_ref[0, :8, :]
    first_ref[8:16, :] = raw_ref[0, :8, :].astype(F32)
    first_ref[16:24, :] = ext_ref[8:16, :]
    first_ref[24:25, :] = rate_row(raw_ref, 0)


def queries_kernel(width, at_ref, taps_ref, key_ref, mix_ref, value_ref, through_ref, memory_ref, *refs):
    pieces, (local_ref, carry_ref, ext_ref) = refs[:-3], refs[-3:]
    chunks, span, depth = key_ref.shape[0], key_ref.shape[1], key_ref.shape[2] // 2
    row, col, _ = grids(span)
    taps = taken(0, head_taps(at_ref, taps_ref, depth), width)
    stage(at_ref, pieces, 1, ext_ref)
    queries = [unit(convolved(ext_ref, 8 - width + c * span, span, taps)) for c in range(chunks)]
    mixed = [
        pair(jnp.where(row >= col, product_t(pair(queries[c]), key_ref[c]), 0.0)) for c in range(chunks)
    ]
    mixed = [pair(product(mixed[c], mix_ref[c])) for c in range(chunks)]
    seen = [pair(queries[c] - product(mixed[c], key_ref[c])) for c in range(chunks)]
    local = [product(mixed[c], value_ref[c]) for c in range(chunks)]
    local_ref[0] = local[0]
    carry_ref[0] = seen[0]
    for c in range(1, chunks):
        local_ref[c] = local[c] + product(seen[c], memory_ref[c - 1])
        carry_ref[c] = pair(product(seen[c], through_ref[c - 1]))


def opening(width, taps, tails, start_ref, ext_ref):
    made = []
    for index in range(3):
        ext_ref[index, :8, :] = tails[8 * index : 8 * index + 8]
        ext_ref[index, 8:, :] = start_ref[8 * index : 8 * index + 8, :]
        made.append(convolved(ext_ref.at[index], 8 - width, 8, taken(index, taps, width)))
    rates = start_ref[24:25, :]
    row = lax.broadcasted_iota(jnp.int32, (8, rates.shape[1]), 0)
    col = lax.broadcasted_iota(jnp.int32, (8, rates.shape[1]), 1)
    strengths = jnp.sum(jnp.where((row == col) & (row < width), rates, 0.0), axis=1, keepdims=True)
    return unit(made[0]), unit(made[1]), made[2], strengths


def finish_kernel(width, at_ref, taps_ref, start_ref, local_ref, carry_ref, memory_ref, gain_ref, out_ref, ext_ref, first_ref):
    depth = local_ref.shape[2]
    later = at_ref[1] > 0
    memory = jnp.where(later, memory_ref[:depth, :], 0.0)
    tails = memory_ref[depth:, :]
    taps = head_taps(at_ref, taps_ref, depth)
    query, key, value, rate = opening(width, taps, tails, start_ref, ext_ref)
    rate = jnp.where(later, rate, 0.0)
    seen = product(pair(jnp.concatenate([key, query], axis=0)), pair(memory))
    delta = rate * (value - seen[:8])
    row = lax.broadcasted_iota(jnp.int32, delta.shape, 0)
    output = seen[8:]
    for t in range(width):
        now = delta[t : t + 1]
        meets = jnp.sum(key * key[t : t + 1], axis=1, keepdims=True)
        delta = jnp.where(row > t, delta - rate * meets * now, delta)
        shown = jnp.sum(query * key[t : t + 1], axis=1, keepdims=True)
        output = jnp.where(row >= t, output + shown * now, output)
    delta = jnp.where(row < width, delta, 0.0)
    turn = (((0,), (0,)), ((), ()))
    key_pair, delta_pair = pair(key), pair(delta)
    both = lax.dot_general(key_pair, delta_pair, turn, preferred_element_type=F32)
    both = both[:depth] + both[depth:]
    memory = pair(memory + both[:, :depth] + both[:, depth:])
    first_ref[...] = output
    gain = gain_ref[...]
    for c in range(local_ref.shape[0]):
        output = local_ref[c] + product(carry_ref[c], memory)
        if c == 0:
            tall = lax.broadcasted_iota(jnp.int32, output.shape, 0)
            opened = jnp.concatenate([first_ref[...]] + [jnp.zeros_like(output[8:])], axis=0)
            output = jnp.where((tall < width) & later, opened, output)
        scale = lax.rsqrt(jnp.mean(output * output, axis=-1, keepdims=True) + 1e-05)
        out_ref[c] = (output * scale * gain).astype(BF16)


def unpack_kernel(piece_ref, out_ref):
    depth = piece_ref.shape[2]
    for head in range(piece_ref.shape[0]):
        out_ref[:, head * depth : (head + 1) * depth] = piece_ref[head]


def compose(later, earlier):
    join = functools.partial(jnp.einsum, "ij,jk->ik", precision=lax.Precision.HIGHEST)
    return jnp.stack([join(later[0], earlier[0]), join(later[0], earlier[1]) + later[1]])


def opening_map(width, taps, tails, first):
    made = []
    for index in range(1, 3):
        rows = jnp.concatenate(
            [tails[8 * index + 8 - width : 8 * index + 8], first[8 * index : 8 * index + width]]
        )
        own = taken(index, taps, width)
        total = sum(rows[tap : tap + width] * own[tap] for tap in range(width + 1))
        made.append(total / (1.0 + jnp.exp(-total)))
    keys = unit(made[0])
    rates = first[24]
    depth = keys.shape[1]
    maps = jnp.stack([jnp.eye(depth, dtype=F32), jnp.zeros((depth, depth), F32)])
    for t in range(width):
        outer = rates[t] * keys[t][:, None]
        one = jnp.stack([jnp.eye(depth, dtype=F32) - outer * keys[t], outer * made[1][t]])
        maps = compose(one, maps)
    return maps


WHOLE = pl.BlockSpec(memory_space=pltpu.VMEM)
SCALAR = pl.BlockSpec(memory_space=pltpu.SMEM)
ANY = pl.BlockSpec(memory_space=pl.ANY)


def call(kernel, name, specs, args, outs, scratch=(), limit=VMEM_LIMIT, out_spec=WHOLE):
    shapes = [jax.ShapeDtypeStruct(shape, dtype) for shape, dtype in outs]
    single = len(shapes) == 1
    return pl.pallas_call(
        kernel,
        out_shape=shapes[0] if single else shapes,
        in_specs=specs,
        out_specs=out_spec if single else [out_spec] * len(shapes),
        scratch_shapes=scratch,
        compiler_params=pltpu.CompilerParams(vmem_limit_bytes=limit),
        name=name,
    )(*args)


def shards(queries, key_rows, value_rows, strength, conv_weight, out_gain):
    taps = conv_weight.shape[1]
    width = taps - 1
    span, heads = strength.shape
    depth = queries.shape[1] // heads
    count = lax.axis_size("seq")
    place = lax.axis_index("seq")
    blocks = count // heads
    assert blocks * heads == count and span == depth and heads & (heads - 1) == 0
    groups = [[b * heads + h for h in range(heads)] for b in range(blocks)]
    block, head = place // heads, place % heads
    at = jnp.stack([head, block]).astype(jnp.int32)

    def share(x):
        return lax.all_to_all(x, "seq", 0, 0, axis_index_groups=groups, tiled=True)

    rows = pltpu.VMEM((span, heads * depth), BF16)
    packed = call(
        pack_kernel,
        "pack",
        [ANY] * 3 + [WHOLE],
        (queries, key_rows, value_rows, strength.T),
        [((heads, span + EXTRA, depth), BF16)] + [((2 * span, depth), BF16)] * heads,
        [rows] * 3
        + [pltpu.VMEM((heads, EXTRA, depth), F32), pltpu.VMEM((heads, EXTRA, depth), BF16)]
        + [pltpu.SemaphoreType.DMA((3,)), pltpu.SemaphoreType.DMA((3 * heads + 1,))],
        limit=VMEM_PACK,
        out_spec=ANY,
    )
    raw = share(packed[0])
    pieces = [packed[1]]
    for slot in range(1, heads):
        pairs = [(i, i ^ slot) for i in range(count)]
        pieces.append(lax.ppermute(packed[1 + slot], "seq", pairs))
    taps_flat = conv_weight.reshape(3 * taps, heads * depth)
    ext = [pltpu.VMEM((heads * span + 8, depth), F32)]
    pairs = ((heads, span, 2 * depth), BF16)
    square = (depth, 2 * depth)
    gain, key, mix, show, factor, through = call(
        functools.partial(keys_kernel, width),
        "keys",
        [SCALAR] + [WHOLE] * 3,
        (at, taps_flat, out_gain.reshape(1, depth), raw),
        [((1, depth), F32)]
        + [pairs] * 3
        + [((sum(map(len, scan_plan(heads))), *square), BF16)]
        + [((heads - (blocks <= 2), *square), BF16)],
        ext + [pltpu.VMEM((heads, *square), BF16)],
    )
    value, memories, final, first = call(
        functools.partial(values_kernel, width),
        "values",
        [SCALAR] + [WHOLE] * (4 + heads),
        (at, taps_flat, raw, show, factor, *pieces),
        [pairs, ((heads - 1, *square), BF16), ((depth + 24, depth), F32), ((32, depth), F32)],
        ext + [pltpu.VMEM((2, 8 * heads, depth), F32)],
    )
    ring = [(i, (i + heads) % count) for i in range(count)]
    memory = lax.ppermute(final, "seq", ring)
    if blocks > 2:
        tails = memory[depth:]
        start = jnp.stack([jnp.eye(depth, dtype=F32), jnp.zeros((depth, depth), F32)])
        whole = through[-1, :, :depth].astype(F32) + through[-1, :, depth:].astype(F32)
        own = lax.dynamic_slice_in_dim(taps_flat, head * depth, depth, 1).astype(F32)
        opened = jnp.where(block > 0, opening_map(width, own, tails, first), start)
        arrived = lax.ppermute(compose(jnp.stack([whole, final[:depth]]), opened), "seq", ring)
        prefix = jnp.where(block > 0, arrived, start)
        reach = 1
        while reach < blocks - 1:
            shift = [(i, (i + reach * heads) % count) for i in range(count)]
            arrived = lax.ppermute(prefix, "seq", shift)
            prefix = jnp.where(block >= reach, compose(prefix, arrived), prefix)
            reach *= 2
        memory = jnp.concatenate([prefix[1], tails])
    local, carry = call(
        functools.partial(queries_kernel, width),
        "queries",
        [SCALAR] + [WHOLE] * (6 + heads),
        (at, taps_flat, key, mix, value, through, memories, *pieces),
        [((heads, span, depth), F32), pairs],
        ext,
    )
    mixed = call(
        functools.partial(finish_kernel, width),
        "finish",
        [SCALAR] + [WHOLE] * 6,
        (at, taps_flat, first, local, carry, memory, gain),
        [((heads, span, depth), BF16)],
        [pltpu.VMEM((3, 16, depth), F32), pltpu.VMEM((8, depth), F32)],
    )
    return call(unpack_kernel, "unpack", [WHOLE], (share(mixed),), [((span, heads * depth), BF16)])


def solution(mesh):
    placed = (
        P(("groups", "seq"), None),
        P(("groups", "seq"), None),
        P(("groups", "seq"), None),
        P(("groups", "seq"), None),
        P(),
        P(),
    )
    return jax.shard_map(
        shards, mesh=mesh, in_specs=placed, out_specs=P(("groups", "seq"), None), check_vma=False
    )
```

```python
import functools

import jax
import jax.numpy as jnp
from jax import lax
from jax.experimental import pallas as pl
from jax.experimental.pallas import tpu as pltpu
from jax.sharding import PartitionSpec as P

EXTRA = 8
FOLD = 32
VMEM_LIMIT = 24 * 1024 * 1024
VMEM_PACK = 66200000
F32 = jnp.float32
BF16 = jnp.bfloat16


def pair(x):
    high = x.astype(BF16)
    return jnp.concatenate([high, (x - high.astype(F32)).astype(BF16)], axis=1)


def product(lhs, rhs):
    both = jnp.dot(lhs, jnp.concatenate([rhs, rhs], axis=0), preferred_element_type=F32)
    half = both.shape[1] // 2
    return both[:, :half] + both[:, half:]


def product_t(lhs, rhs):
    k = rhs.shape[1] // 2
    high, low = rhs[:, :k], rhs[:, k:]
    rhs = jnp.concatenate(
        [jnp.concatenate([high, high], axis=1), jnp.concatenate([low, low], axis=1)], axis=0
    )
    both = lax.dot_general(lhs, rhs, (((1,), (1,)), ((), ())), preferred_element_type=F32)
    half = both.shape[1] // 2
    return both[:, :half] + both[:, half:]


def position(heads):
    place = lax.axis_index("seq")
    return lax.rem(place, heads), lax.div(place, heads)


def pack_kernel(q_hbm, k_hbm, v_hbm, rate_hbm, taps_hbm, gain_hbm, keys_hbm, *refs):
    pieces, small_hbm = refs[:-12], refs[-12]
    q_ref, k_ref, v_ref, rate_ref, taps_ref, gain_ref, parts_ref, extra_ref, small_ref, in_sems, out_sems = refs[-11:]
    heads, span = rate_ref.shape
    depth = q_ref.shape[1] // heads
    own = position(heads)[0]
    arrivals = (
        (rate_hbm, rate_ref),
        (k_hbm, k_ref),
        (v_hbm, v_ref),
        (q_hbm, q_ref),
        (taps_hbm, taps_ref),
        (gain_hbm, gain_ref),
    )
    arriving = [pltpu.make_async_copy(*ends, in_sems.at[index]) for index, ends in enumerate(arrivals)]
    for copy in arriving:
        copy.start()
    leaving = []

    def leave(source, target):
        leaving.append(pltpu.make_async_copy(source, target, out_sems.at[len(leaving)]))
        leaving[-1].start()

    parts_ref[...] = jnp.zeros_like(parts_ref)
    arriving[0].wait()
    rate = rate_ref[...]
    for part in range(3):
        high = rate.astype(BF16).astype(F32)
        for head in range(heads):
            parts_ref[head, part : part + 1, :] = high[head : head + 1]
        rate = rate - high
    extra_ref[...] = parts_ref[...].astype(BF16)
    arriving[1].wait()
    for head in range(heads):
        leave(k_ref.at[:, head * depth : (head + 1) * depth], keys_hbm.at[head, :span, :])
    leave(extra_ref, keys_hbm.at[:, span:, :])
    own_lanes = pl.ds(pl.multiple_of(own * depth, depth), depth)
    for index, source in enumerate((v_ref, q_ref)):
        arriving[2 + index].wait()
        for slot in range(heads):
            lanes = pl.ds(pl.multiple_of((own ^ slot) * depth, depth), depth)
            leave(source.at[:, lanes], pieces[slot].at[index * span : (index + 1) * span, :])
    arriving[4].wait()
    arriving[5].wait()
    count = taps_ref.shape[1]
    for index in range(3):
        small_ref[index * count : (index + 1) * count, :] = taps_ref[index, :, own_lanes].astype(F32)
    small_ref[3 * count : 3 * count + 1, :] = gain_ref[...]
    leave(small_ref, small_hbm)
    for copy in leaving:
        copy.wait()


def convolved(ext_ref, first, rows, taps):
    total = ext_ref[first : first + rows, :] * taps[:1]
    for tap in range(1, taps.shape[0]):
        total += ext_ref[first + tap : first + tap + rows, :] * taps[tap : tap + 1]
    return total / (1.0 + jnp.exp(-total))


def stage_keys(raw_ref, ext_ref):
    span = raw_ref.shape[1] - EXTRA
    ext_ref[:8, :] = jnp.zeros_like(ext_ref[:8, :])
    for c in range(raw_ref.shape[0]):
        ext_ref[8 + c * span : 8 + (c + 1) * span, :] = raw_ref[c, :span, :].astype(F32)


def stage(pieces, index, ext_ref):
    span = pieces[0].shape[0] // 2
    ext_ref[:8, :] = jnp.zeros_like(ext_ref[:8, :])
    for slot, piece in enumerate(pieces):
        rows = pl.ds(pl.multiple_of(8 + (position(len(pieces))[0] ^ slot) * span, 8), span)
        ext_ref[rows, :] = piece[index * span : (index + 1) * span, :].astype(F32)


def taken(index, taps, width):
    return taps[index * (width + 1) : (index + 1) * (width + 1)]


def rate_row(raw_ref, c):
    parts = raw_ref[c, raw_ref.shape[1] - EXTRA :, :].astype(F32)
    return parts[:1] + parts[1:2] + parts[2:3]


def unit(x):
    return x * lax.rsqrt(jnp.sum(x * x, axis=-1, keepdims=True) + 1e-06)


def grids(span):
    row = lax.broadcasted_iota(jnp.int32, (span, span), 0)
    col = lax.broadcasted_iota(jnp.int32, (span, span), 1)
    return row, col, (row == col).astype(F32)


def scan_plan(chunks):
    plan, reach = [], 1
    while reach < chunks:
        plan.append([(c, (c // reach) * reach - 1) for c in range(chunks) if c // reach % 2])
        reach *= 2
    return plan


def scan_updates(chunks):
    wanted, updates = set(), []
    for level in reversed(scan_plan(chunks)):
        grown = [(c, earlier) for c, earlier in level if c in wanted]
        updates.append({c for c, _ in grown})
        wanted |= {c for c, _ in level} | {earlier for _, earlier in grown}
    return updates[::-1]


def scan_index(chunks):
    return {pair_: at for at, pair_ in enumerate(p for level in scan_plan(chunks) for p in level)}


def prefixes(chunks, first, factor, join):
    maps, index = [first], scan_index(1 << (chunks - 1).bit_length())
    for c in range(1, chunks):
        earlier = (1 << (c.bit_length() - 1)) - 1
        maps.append(join(factor(index[c, earlier]), maps[earlier]))
    return maps


def fold_product(lhs, rhs, width):
    lanes = rhs.shape[1]
    if width == lanes:
        return product(lhs, pair(rhs))
    at = lax.broadcasted_iota(jnp.int32, rhs.shape, 1) // width
    high = rhs.astype(BF16).astype(F32)
    parts = (high, rhs - high)
    rows = [
        jnp.concatenate([jnp.where(at == i, part, 0.0).astype(BF16) for part in parts], axis=1)
        for i in range(lanes // width)
    ]
    both = jnp.dot(lhs, jnp.concatenate(rows + rows, axis=0), preferred_element_type=F32)
    return both[:, :lanes] + both[:, lanes:]


def inverse_of(lowers):
    span = lowers[0].shape[0]
    width = FOLD
    lane = lax.broadcasted_iota(jnp.int32, (width, span), 1)
    inner = lowers
    while inner[0].shape[0] > width:
        half = inner[0].shape[0] // 2
        side = lax.broadcasted_iota(jnp.int32, (half, span), 1) // half % 2
        inner = [jnp.where(side == 0, x[:half], x[half:]) for x in inner]
    row = lax.broadcasted_iota(jnp.int32, (width, span), 0)
    col = lane % width
    done = [(row == col).astype(F32) - jnp.where((row ^ col) == 1, x, 0.0) for x in inner]
    size = 2
    while size < span:
        wide = min(4 * size, span)
        if wide > width:
            side = lax.broadcasted_iota(jnp.int32, (width, span), 1) // width
            done = [
                jnp.concatenate([jnp.where(side == i, x, 0.0) for i in range(span // width)], axis=0) for x in done
            ]
            width, inner = span, lowers
            row = lax.broadcasted_iota(jnp.int32, (width, span), 0)
            col = lax.broadcasted_iota(jnp.int32, (width, span), 1)
        pick = (row // wide == col // wide) & (row // size != col // size)
        pairs = [pair(x) for x in done]
        z = [fold_product(y, jnp.where(pick, x, 0.0), width) for x, y in zip(inner, pairs)]
        pairs = [pair(x) for x in z]
        square = [fold_product(y, x, width) for x, y in zip(z, pairs)]
        done = [x - fold_product(y, x, width) for x, y in zip(done, pairs)]
        done = [x + fold_product(pair(y), x, width) for x, y in zip(done, square)]
        size = wide
    return done


def keys_kernel(width, small_ref, raw_ref, key_ref, mix_ref, show_ref, factor_ref, open_ref, ext_ref, run_ref):
    chunks, depth = raw_ref.shape[0], raw_ref.shape[2]
    span = raw_ref.shape[1] - EXTRA
    row, col, eye = grids(span)
    taps = taken(1, small_ref[...], width)
    stage_keys(raw_ref, ext_ref)
    lowers, rates, turned = [], [], []
    for c in range(chunks):
        key = unit(convolved(ext_ref, 8 - width + c * span, span, taps))
        rates.append(rate_row(raw_ref, c))
        if c == 0:
            rates[c] = jnp.where((col[:1] < width) & (position(chunks)[1] > 0), 0.0, rates[c])
        rate = jnp.sum(eye * rates[c], axis=1, keepdims=True)
        key_pair = pair(key)
        key_ref[c] = key_pair
        turned.append(pair(key.T))
        lowers.append(jnp.where(row > col, rate * product_t(key_pair, key_pair), 0.0))
    inverses = inverse_of(lowers)
    for c in range(chunks):
        mix = pair(inverses[c] * rates[c])
        mix_ref[c] = mix
        show = pair(product(turned[c], mix))
        show_ref[c] = show
        run_ref[c] = pair(eye - product(show, key_ref[c]))
    open_ref[...] = run_ref[0]
    at = 0
    for level, grown in zip(scan_plan(chunks), scan_updates(chunks)):
        for c, earlier in level:
            factor_ref[at] = run_ref[c]
            at += 1
        for c, earlier in level:
            if c in grown:
                run_ref[c] = pair(product(run_ref[c], run_ref[earlier]))


def values_kernel(width, small_ref, raw_ref, show_ref, factor_ref, *refs):
    pieces, (value_ref, memory_ref, final_ref, first_ref, ext_ref, edge_ref) = refs[:-6], refs[-6:]
    chunks, depth = raw_ref.shape[0], raw_ref.shape[2]
    span = raw_ref.shape[1] - EXTRA
    taps = taken(2, small_ref[...], width)
    stage(pieces, 0, ext_ref)
    states = []
    for c in range(chunks):
        value = pair(convolved(ext_ref, 8 - width + c * span, span, taps))
        value_ref[c] = value
        states.append(product(show_ref[c], value))
    at = 0
    for level in scan_plan(chunks):
        for c, earlier in level:
            states[c] = states[c] + product(factor_ref[at], pair(states[earlier]))
            at += 1
    for c in range(chunks - 1):
        memory_ref[c] = pair(states[c])
    final_ref[:depth, :] = states[chunks - 1]
    for slot, piece in enumerate(pieces):
        chunk = position(chunks)[0] ^ slot
        edge_ref[0, pl.ds(pl.multiple_of(8 * chunk, 8), 8), :] = piece[span : span + 8, :].astype(F32)
        edge_ref[1, pl.ds(pl.multiple_of(8 * chunk, 8), 8), :] = piece[2 * span - 8 :, :].astype(F32)
    last = 8 * (chunks - 1)
    final_ref[depth : depth + 8, :] = edge_ref[1, last : last + 8, :]
    final_ref[depth + 8 : depth + 16, :] = raw_ref[chunks - 1, span - 8 : span, :].astype(F32)
    final_ref[depth + 16 : depth + 24, :] = ext_ref[chunks * span : chunks * span + 8, :]
    first_ref[:8, :] = edge_ref[0, :8, :]
    first_ref[8:16, :] = raw_ref[0, :8, :].astype(F32)
    first_ref[16:24, :] = ext_ref[8:16, :]
    first_ref[24:25, :] = rate_row(raw_ref, 0)


def queries_kernel(width, small_ref, key_ref, mix_ref, value_ref, open_ref, factor_ref, memory_ref, *refs):
    pieces, (local_ref, carry_ref, ext_ref) = refs[:-3], refs[-3:]
    chunks, span, depth = key_ref.shape[0], key_ref.shape[1], key_ref.shape[2] // 2
    row, col, _ = grids(span)
    taps = taken(0, small_ref[...], width)
    stage(pieces, 1, ext_ref)
    queries = [unit(convolved(ext_ref, 8 - width + c * span, span, taps)) for c in range(chunks)]
    mixed = [
        pair(jnp.where(row >= col, product_t(pair(queries[c]), key_ref[c]), 0.0)) for c in range(chunks)
    ]
    mixed = [pair(product(mixed[c], mix_ref[c])) for c in range(chunks)]
    seen = [pair(queries[c] - product(mixed[c], key_ref[c])) for c in range(chunks)]
    local = [product(mixed[c], value_ref[c]) for c in range(chunks)]
    local_ref[0] = local[0]
    carry_ref[0] = seen[0]
    through = prefixes(
        chunks - 1, open_ref[...], lambda at: factor_ref[at], lambda x, y: pair(product(x, y))
    )
    for c in range(1, chunks):
        local_ref[c] = local[c] + product(seen[c], memory_ref[c - 1])
        carry_ref[c] = pair(product(seen[c], through[c - 1]))


def opening(width, taps, tails, start_ref, ext_ref):
    made = []
    for index in range(3):
        ext_ref[index, :8, :] = tails[8 * index : 8 * index + 8]
        ext_ref[index, 8:, :] = start_ref[8 * index : 8 * index + 8, :]
        made.append(convolved(ext_ref.at[index], 8 - width, 8, taken(index, taps, width)))
    rates = start_ref[24:25, :]
    row = lax.broadcasted_iota(jnp.int32, (8, rates.shape[1]), 0)
    col = lax.broadcasted_iota(jnp.int32, (8, rates.shape[1]), 1)
    strengths = jnp.sum(jnp.where((row == col) & (row < width), rates, 0.0), axis=1, keepdims=True)
    return unit(made[0]), unit(made[1]), made[2], strengths


def finish_kernel(width, small_ref, start_ref, local_ref, carry_ref, memory_ref, out_ref, ext_ref, first_ref):
    depth = local_ref.shape[2]
    later = position(local_ref.shape[0])[1] > 0
    memory = jnp.where(later, memory_ref[:depth, :], 0.0)
    tails = memory_ref[depth:, :]
    taps = small_ref[...]
    query, key, value, rate = opening(width, taps, tails, start_ref, ext_ref)
    rate = jnp.where(later, rate, 0.0)
    seen = product(pair(jnp.concatenate([key, query], axis=0)), pair(memory))
    delta = rate * (value - seen[:8])
    row = lax.broadcasted_iota(jnp.int32, delta.shape, 0)
    output = seen[8:]
    for t in range(width):
        now = delta[t : t + 1]
        meets = jnp.sum(key * key[t : t + 1], axis=1, keepdims=True)
        delta = jnp.where(row > t, delta - rate * meets * now, delta)
        shown = jnp.sum(query * key[t : t + 1], axis=1, keepdims=True)
        output = jnp.where(row >= t, output + shown * now, output)
    delta = jnp.where(row < width, delta, 0.0)
    turn = (((0,), (0,)), ((), ()))
    key_pair, delta_pair = pair(key), pair(delta)
    both = lax.dot_general(key_pair, delta_pair, turn, preferred_element_type=F32)
    both = both[:depth] + both[depth:]
    memory = pair(memory + both[:, :depth] + both[:, depth:])
    first_ref[...] = output
    gain = small_ref[3 * (width + 1) : 3 * (width + 1) + 1, :]
    for c in range(local_ref.shape[0]):
        output = local_ref[c] + product(carry_ref[c], memory)
        if c == 0:
            tall = lax.broadcasted_iota(jnp.int32, output.shape, 0)
            opened = jnp.concatenate([first_ref[...]] + [jnp.zeros_like(output[8:])], axis=0)
            output = jnp.where((tall < width) & later, opened, output)
        scale = lax.rsqrt(jnp.mean(output * output, axis=-1, keepdims=True) + 1e-05)
        out_ref[c] = (output * scale * gain).astype(BF16)


def unpack_kernel(piece_ref, out_ref):
    depth = piece_ref.shape[2]
    for head in range(piece_ref.shape[0]):
        out_ref[:, head * depth : (head + 1) * depth] = piece_ref[head]


def compose(later, earlier):
    join = functools.partial(jnp.einsum, "ij,jk->ik", precision=lax.Precision.HIGHEST)
    return jnp.stack([join(later[0], earlier[0]), join(later[0], earlier[1]) + later[1]])


def opening_map(width, taps, tails, first):
    made = []
    for index in range(1, 3):
        rows = jnp.concatenate(
            [tails[8 * index + 8 - width : 8 * index + 8], first[8 * index : 8 * index + width]]
        )
        own = taken(index, taps, width)
        total = sum(rows[tap : tap + width] * own[tap] for tap in range(width + 1))
        made.append(total / (1.0 + jnp.exp(-total)))
    keys = unit(made[0])
    rates = first[24]
    depth = keys.shape[1]
    maps = jnp.stack([jnp.eye(depth, dtype=F32), jnp.zeros((depth, depth), F32)])
    for t in range(width):
        outer = rates[t] * keys[t][:, None]
        one = jnp.stack([jnp.eye(depth, dtype=F32) - outer * keys[t], outer * made[1][t]])
        maps = compose(one, maps)
    return maps


WHOLE = pl.BlockSpec(memory_space=pltpu.VMEM)
ANY = pl.BlockSpec(memory_space=pl.ANY)


def call(kernel, name, specs, args, outs, scratch=(), limit=VMEM_LIMIT, out_spec=WHOLE):
    shapes = [jax.ShapeDtypeStruct(shape, dtype) for shape, dtype in outs]
    single = len(shapes) == 1
    return pl.pallas_call(
        kernel,
        out_shape=shapes[0] if single else shapes,
        in_specs=specs,
        out_specs=out_spec if single else [out_spec] * len(shapes),
        scratch_shapes=scratch,
        compiler_params=pltpu.CompilerParams(vmem_limit_bytes=limit),
        name=name,
    )(*args)


def shards(queries, key_rows, value_rows, strength, conv_weight, out_gain):
    taps = conv_weight.shape[1]
    width = taps - 1
    span, heads = strength.shape
    depth = queries.shape[1] // heads
    count = lax.axis_size("seq")
    place = lax.axis_index("seq")
    blocks = count // heads
    assert blocks * heads == count and span == depth and heads & (heads - 1) == 0
    groups = [[b * heads + h for h in range(heads)] for b in range(blocks)]
    block = place // heads

    def share(x):
        return lax.all_to_all(x, "seq", 0, 0, axis_index_groups=groups, tiled=True)

    rows = pltpu.VMEM((span, heads * depth), BF16)
    small = ((16, depth), F32)
    assert 3 * taps < small[0][0]
    packed = call(
        pack_kernel,
        "pack",
        [ANY] * 6,
        (queries, key_rows, value_rows, strength.T, conv_weight, out_gain.reshape(1, depth)),
        [((heads, span + EXTRA, depth), BF16)] + [((2 * span, depth), BF16)] * heads + [small],
        [rows] * 3
        + [pltpu.VMEM((heads, span), F32), pltpu.VMEM(conv_weight.shape, BF16), pltpu.VMEM((1, depth), F32)]
        + [pltpu.VMEM((heads, EXTRA, depth), F32), pltpu.VMEM((heads, EXTRA, depth), BF16), pltpu.VMEM(*small)]
        + [pltpu.SemaphoreType.DMA((6,)), pltpu.SemaphoreType.DMA((3 * heads + 2,))],
        limit=VMEM_PACK,
        out_spec=ANY,
    )
    small = packed[-1]
    raw = share(packed[0])
    pieces = [packed[1]]
    for slot in range(1, heads):
        pairs = [(i, i ^ slot) for i in range(count)]
        pieces.append(lax.ppermute(packed[1 + slot], "seq", pairs))
    ext = [pltpu.VMEM((heads * span + 8, depth), F32)]
    pairs = ((heads, span, 2 * depth), BF16)
    square = (depth, 2 * depth)
    key, mix, show, factor, opener = call(
        functools.partial(keys_kernel, width),
        "keys",
        [WHOLE] * 2,
        (small, raw),
        [pairs] * 3 + [((len(scan_index(heads)), *square), BF16), (square, BF16)],
        ext + [pltpu.VMEM((heads, *square), BF16)],
    )
    value, memories, final, first = call(
        functools.partial(values_kernel, width),
        "values",
        [WHOLE] * (4 + heads),
        (small, raw, show, factor, *pieces),
        [pairs, ((heads - 1, *square), BF16), ((depth + 24, depth), F32), ((32, depth), F32)],
        ext + [pltpu.VMEM((2, 8 * heads, depth), F32)],
    )
    ring = [(i, (i + heads) % count) for i in range(count)]
    memory = lax.ppermute(final, "seq", ring)
    if blocks > 2:
        tails = memory[depth:]
        start = jnp.stack([jnp.eye(depth, dtype=F32), jnp.zeros((depth, depth), F32)])

        def joined(x):
            return x[:, :depth].astype(F32) + x[:, depth:].astype(F32)

        join = functools.partial(jnp.matmul, precision=lax.Precision.HIGHEST)
        whole = prefixes(heads, joined(opener), lambda at: joined(factor[at]), join)[-1]
        opened = jnp.where(block > 0, opening_map(width, small, tails, first), start)
        arrived = lax.ppermute(compose(jnp.stack([whole, final[:depth]]), opened), "seq", ring)
        prefix = jnp.where(block > 0, arrived, start)
        reach = 1
        while reach < blocks - 1:
            shift = [(i, (i + reach * heads) % count) for i in range(count)]
            arrived = lax.ppermute(prefix, "seq", shift)
            prefix = jnp.where(block >= reach, compose(prefix, arrived), prefix)
            reach *= 2
        memory = jnp.concatenate([prefix[1], tails])
    local, carry = call(
        functools.partial(queries_kernel, width),
        "queries",
        [WHOLE] * (7 + heads),
        (small, key, mix, value, opener, factor, memories, *pieces),
        [((heads, span, depth), F32), pairs],
        ext,
    )
    mixed = call(
        functools.partial(finish_kernel, width),
        "finish",
        [WHOLE] * 5,
        (small, first, local, carry, memory),
        [((heads, span, depth), BF16)],
        [pltpu.VMEM((3, 16, depth), F32), pltpu.VMEM((8, depth), F32)],
    )
    return call(unpack_kernel, "unpack", [WHOLE], (share(mixed),), [((span, heads * depth), BF16)])


def solution(mesh):
    placed = (
        P(("groups", "seq"), None),
        P(("groups", "seq"), None),
        P(("groups", "seq"), None),
        P(("groups", "seq"), None),
        P(),
        P(),
    )
    return jax.shard_map(
        shards, mesh=mesh, in_specs=placed, out_specs=P(("groups", "seq"), None), check_vma=False
    )
```

```python
import functools

import jax
import jax.numpy as jnp
from jax import lax
from jax.experimental import pallas as pl
from jax.experimental.pallas import tpu as pltpu
from jax.sharding import PartitionSpec as P


EXTRA = 8
FOLD = 32
VMEM_LIMIT = 24 * 1024 * 1024
VMEM_PACK = 66200000
F32 = jnp.float32
BF16 = jnp.bfloat16


def pair(x):
    high = x.astype(BF16)
    return jnp.concatenate([high, (x - high.astype(F32)).astype(BF16)], axis=1)


def product(lhs, rhs):
    both = jnp.dot(lhs, jnp.concatenate([rhs, rhs], axis=0), preferred_element_type=F32)
    half = both.shape[1] // 2
    return both[:, :half] + both[:, half:]


def product_t(lhs, rhs):
    k = rhs.shape[1] // 2
    high, low = rhs[:, :k], rhs[:, k:]
    rhs = jnp.concatenate(
        [jnp.concatenate([high, high], axis=1), jnp.concatenate([low, low], axis=1)], axis=0
    )
    both = lax.dot_general(lhs, rhs, (((1,), (1,)), ((), ())), preferred_element_type=F32)
    half = both.shape[1] // 2
    return both[:, :half] + both[:, half:]


def position(heads):
    place = lax.axis_index("seq")
    return lax.rem(place, heads), lax.div(place, heads)


def pack_kernel(width, q_hbm, k_hbm, v_hbm, rate_hbm, taps_hbm, gain_hbm, keys_hbm, *refs):
    pieces, small_hbm = refs[:-12], refs[-12]
    q_ref, k_ref, v_ref, rate_ref, taps_ref, gain_ref, parts_ref, extra_ref, small_ref, in_sems, out_sems = refs[-11:]
    heads, span = rate_ref.shape
    depth = q_ref.shape[1] // heads
    own = position(heads)[0]
    arrivals = (
        (rate_hbm, rate_ref),
        (k_hbm, k_ref),
        (v_hbm, v_ref),
        (q_hbm, q_ref),
        (taps_hbm, taps_ref),
        (gain_hbm, gain_ref),
    )
    arriving = [pltpu.make_async_copy(*ends, in_sems.at[index]) for index, ends in enumerate(arrivals)]
    for copy in arriving:
        copy.start()
    leaving = []

    def leave(source, target):
        leaving.append(pltpu.make_async_copy(source, target, out_sems.at[len(leaving)]))
        leaving[-1].start()

    parts_ref[...] = jnp.zeros_like(parts_ref)
    arriving[0].wait()
    rate = rate_ref[...]
    for part in range(3):
        high = rate.astype(BF16).astype(F32)
        for head in range(heads):
            parts_ref[head, part : part + 1, :] = high[head : head + 1]
        rate = rate - high
    for index, source in enumerate((k_ref, v_ref)):
        arriving[1 + index].wait()
        for head in range(heads):
            lanes = slice(head * depth, (head + 1) * depth)
            leave(source.at[:, lanes], keys_hbm.at[head, index * span : (index + 1) * span, :])
    arriving[3].wait()
    own_lanes = pl.ds(pl.multiple_of(own * depth, depth), depth)
    for slot in range(heads):
        lanes = pl.ds(pl.multiple_of((own ^ slot) * depth, depth), depth)
        leave(q_ref.at[:, lanes], pieces[slot])
        tail = q_ref[span - width :, slot * depth : (slot + 1) * depth]
        parts_ref[slot, 3 : 3 + width, :] = tail.astype(F32)
    extra_ref[...] = parts_ref[...].astype(BF16)
    leave(extra_ref, keys_hbm.at[:, 2 * span :, :])
    arriving[4].wait()
    arriving[5].wait()
    count = taps_ref.shape[1]
    for index in range(3):
        small_ref[index * count : (index + 1) * count, :] = taps_ref[index, :, own_lanes].astype(F32)
    small_ref[3 * count : 3 * count + 1, :] = gain_ref[...]
    leave(small_ref, small_hbm)
    for copy in leaving:
        copy.wait()


def convolved(ext_ref, first, rows, taps):
    total = ext_ref[first : first + rows, :] * taps[:1]
    for tap in range(1, taps.shape[0]):
        total += ext_ref[first + tap : first + tap + rows, :] * taps[tap : tap + 1]
    return total / (1.0 + jnp.exp(-total))


def span_of(raw_ref):
    return (raw_ref.shape[1] - EXTRA) // 2


def stage_rows(raw_ref, index, ext_ref):
    span = span_of(raw_ref)
    ext_ref[:8, :] = jnp.zeros_like(ext_ref[:8, :])
    for c in range(raw_ref.shape[0]):
        rows = raw_ref[c, index * span : (index + 1) * span, :]
        ext_ref[8 + c * span : 8 + (c + 1) * span, :] = rows.astype(F32)


def stage_pieces(pieces, ext_ref):
    span = pieces[0].shape[0]
    ext_ref[:8, :] = jnp.zeros_like(ext_ref[:8, :])
    for slot, piece in enumerate(pieces):
        rows = pl.ds(pl.multiple_of(8 + (position(len(pieces))[0] ^ slot) * span, 8), span)
        ext_ref[rows, :] = piece[...].astype(F32)


def taken(index, taps, width):
    return taps[index * (width + 1) : (index + 1) * (width + 1)]


def rate_row(raw_ref, c):
    parts = raw_ref[c, raw_ref.shape[1] - EXTRA :, :].astype(F32)
    return parts[:1] + parts[1:2] + parts[2:3]


def unit(x):
    return x * lax.rsqrt(jnp.sum(x * x, axis=-1, keepdims=True) + 1e-06)


def grids(span):
    row = lax.broadcasted_iota(jnp.int32, (span, span), 0)
    col = lax.broadcasted_iota(jnp.int32, (span, span), 1)
    return row, col, (row == col).astype(F32)


def scan_plan(chunks):
    plan, reach = [], 1
    while reach < chunks:
        plan.append([(c, (c // reach) * reach - 1) for c in range(chunks) if c // reach % 2])
        reach *= 2
    return plan


def scan_updates(chunks):
    wanted, updates = set(), []
    for level in reversed(scan_plan(chunks)):
        grown = [(c, earlier) for c, earlier in level if c in wanted]
        updates.append({c for c, _ in grown})
        wanted |= {c for c, _ in level} | {earlier for _, earlier in grown}
    return updates[::-1]


def scan_index(chunks):
    return {pair_: at for at, pair_ in enumerate(p for level in scan_plan(chunks) for p in level)}


def prefixes(chunks, first, factor, join):
    maps, index = [first], scan_index(1 << (chunks - 1).bit_length())
    for c in range(1, chunks):
        earlier = (1 << (c.bit_length() - 1)) - 1
        maps.append(join(factor(index[c, earlier]), maps[earlier]))
    return maps


def fold_product(lhs, rhs, width):
    lanes = rhs.shape[1]
    if width == lanes:
        return product(lhs, pair(rhs))
    at = lax.broadcasted_iota(jnp.int32, rhs.shape, 1) // width
    high = rhs.astype(BF16).astype(F32)
    parts = (high, rhs - high)
    rows = [
        jnp.concatenate([jnp.where(at == i, part, 0.0).astype(BF16) for part in parts], axis=1)
        for i in range(lanes // width)
    ]
    both = jnp.dot(lhs, jnp.concatenate(rows + rows, axis=0), preferred_element_type=F32)
    return both[:, :lanes] + both[:, lanes:]


def inverse_of(lowers):
    span = lowers[0].shape[0]
    width = FOLD
    lane = lax.broadcasted_iota(jnp.int32, (width, span), 1)
    inner = lowers
    while inner[0].shape[0] > width:
        half = inner[0].shape[0] // 2
        side = lax.broadcasted_iota(jnp.int32, (half, span), 1) // half % 2
        inner = [jnp.where(side == 0, x[:half], x[half:]) for x in inner]
    row = lax.broadcasted_iota(jnp.int32, (width, span), 0)
    col = lane % width
    done = [(row == col).astype(F32) - jnp.where((row ^ col) == 1, x, 0.0) for x in inner]
    size = 2
    while size < span:
        wide = min(4 * size, span)
        if wide > width:
            side = lax.broadcasted_iota(jnp.int32, (width, span), 1) // width
            done = [
                jnp.concatenate([jnp.where(side == i, x, 0.0) for i in range(span // width)], axis=0) for x in done
            ]
            width, inner = span, lowers
            row = lax.broadcasted_iota(jnp.int32, (width, span), 0)
            col = lax.broadcasted_iota(jnp.int32, (width, span), 1)
        pick = (row // wide == col // wide) & (row // size != col // size)
        pairs = [pair(x) for x in done]
        z = [fold_product(y, jnp.where(pick, x, 0.0), width) for x, y in zip(inner, pairs)]
        pairs = [pair(x) for x in z]
        square = [fold_product(y, x, width) for x, y in zip(z, pairs)]
        done = [x - fold_product(y, x, width) for x, y in zip(done, pairs)]
        done = [x + fold_product(pair(y), x, width) for x, y in zip(done, square)]
        size = wide
    return done


def keys_kernel(width, small_ref, raw_ref, key_ref, mix_ref, show_ref, factor_ref, open_ref, ext_ref, run_ref):
    chunks = raw_ref.shape[0]
    span = span_of(raw_ref)
    row, col, eye = grids(span)
    taps = taken(1, small_ref[...], width)
    stage_rows(raw_ref, 0, ext_ref)
    lowers, rates, turned = [], [], []
    for c in range(chunks):
        key = unit(convolved(ext_ref, 8 - width + c * span, span, taps))
        rates.append(rate_row(raw_ref, c))
        if c == 0:
            rates[c] = jnp.where((col[:1] < width) & (position(chunks)[1] > 0), 0.0, rates[c])
        rate = jnp.sum(eye * rates[c], axis=1, keepdims=True)
        key_pair = pair(key)
        key_ref[c] = key_pair
        turned.append(pair(key.T))
        lowers.append(jnp.where(row > col, rate * product_t(key_pair, key_pair), 0.0))
    inverses = inverse_of(lowers)
    for c in range(chunks):
        mix = pair(inverses[c] * rates[c])
        mix_ref[c] = mix
        show = pair(product(turned[c], mix))
        show_ref[c] = show
        run_ref[c] = pair(eye - product(show, key_ref[c]))
    open_ref[...] = run_ref[0]
    at = 0
    for level, grown in zip(scan_plan(chunks), scan_updates(chunks)):
        for c, earlier in level:
            factor_ref[at] = run_ref[c]
            at += 1
        for c, earlier in level:
            if c in grown:
                run_ref[c] = pair(product(run_ref[c], run_ref[earlier]))


def values_kernel(width, small_ref, raw_ref, show_ref, factor_ref, value_ref, memory_ref, final_ref, first_ref, ext_ref):
    chunks, depth = raw_ref.shape[0], raw_ref.shape[2]
    span = span_of(raw_ref)
    taps = taken(2, small_ref[...], width)
    stage_rows(raw_ref, 1, ext_ref)
    states = []
    for c in range(chunks):
        value = pair(convolved(ext_ref, 8 - width + c * span, span, taps))
        value_ref[c] = value
        states.append(product(show_ref[c], value))
    at = 0
    for level in scan_plan(chunks):
        for c, earlier in level:
            states[c] = states[c] + product(factor_ref[at], pair(states[earlier]))
            at += 1
    for c in range(chunks - 1):
        memory_ref[c] = pair(states[c])
    final_ref[:depth, :] = states[chunks - 1]
    extra = raw_ref[chunks - 1, 2 * span :, :].astype(F32)
    final_ref[depth : depth + width, :] = extra[3 : 3 + width]
    for index in range(2):
        tail = raw_ref[chunks - 1, (index + 1) * span - width : (index + 1) * span, :]
        final_ref[depth + (index + 1) * width : depth + (index + 2) * width, :] = tail.astype(F32)
        first_ref[8 * index : 8 * index + 8, :] = raw_ref[0, index * span : index * span + 8, :].astype(F32)
    first_ref[16:17, :] = rate_row(raw_ref, 0)


def queries_kernel(width, small_ref, key_ref, mix_ref, value_ref, open_ref, factor_ref, memory_ref, *refs):
    pieces, (local_ref, carry_ref, first_ref, ext_ref) = refs[:-4], refs[-4:]
    chunks, span = key_ref.shape[0], key_ref.shape[1]
    row, col, _ = grids(span)
    taps = taken(0, small_ref[...], width)
    stage_pieces(pieces, ext_ref)
    first_ref[...] = ext_ref[8:16, :]
    queries = [unit(convolved(ext_ref, 8 - width + c * span, span, taps)) for c in range(chunks)]
    mixed = [
        pair(jnp.where(row >= col, product_t(pair(queries[c]), key_ref[c]), 0.0)) for c in range(chunks)
    ]
    mixed = [pair(product(mixed[c], mix_ref[c])) for c in range(chunks)]
    seen = [pair(queries[c] - product(mixed[c], key_ref[c])) for c in range(chunks)]
    local = [product(mixed[c], value_ref[c]) for c in range(chunks)]
    local_ref[0] = local[0]
    carry_ref[0] = seen[0]
    through = prefixes(
        chunks - 1, open_ref[...], lambda at: factor_ref[at], lambda x, y: pair(product(x, y))
    )
    for c in range(1, chunks):
        local_ref[c] = local[c] + product(seen[c], memory_ref[c - 1])
        carry_ref[c] = pair(product(seen[c], through[c - 1]))


def opening(width, taps, tails, starts, rates, ext_ref):
    made = []
    for index in range(3):
        ext_ref[index, 8 - width : 8, :] = tails[width * index : width * index + width]
        ext_ref[index, 8:, :] = starts[index]
        made.append(convolved(ext_ref.at[index], 8 - width, 8, taken(index, taps, width)))
    row = lax.broadcasted_iota(jnp.int32, (8, rates.shape[1]), 0)
    col = lax.broadcasted_iota(jnp.int32, (8, rates.shape[1]), 1)
    strengths = jnp.sum(jnp.where((row == col) & (row < width), rates, 0.0), axis=1, keepdims=True)
    return unit(made[0]), unit(made[1]), made[2], strengths


def finish_kernel(width, small_ref, query_ref, first_ref, local_ref, carry_ref, memory_ref, out_ref, ext_ref, opened_ref):
    depth = local_ref.shape[2]
    later = position(local_ref.shape[0])[1] > 0
    memory = jnp.where(later, memory_ref[:depth, :], 0.0)
    tails = memory_ref[depth:, :]
    taps = small_ref[...]
    starts = (query_ref[...], first_ref[:8, :], first_ref[8:16, :])
    query, key, value, rate = opening(width, taps, tails, starts, first_ref[16:17, :], ext_ref)
    rate = jnp.where(later, rate, 0.0)
    seen = product(pair(jnp.concatenate([key, query], axis=0)), pair(memory))
    delta = rate * (value - seen[:8])
    row = lax.broadcasted_iota(jnp.int32, delta.shape, 0)
    output = seen[8:]
    for t in range(width):
        now = delta[t : t + 1]
        meets = jnp.sum(key * key[t : t + 1], axis=1, keepdims=True)
        delta = jnp.where(row > t, delta - rate * meets * now, delta)
        shown = jnp.sum(query * key[t : t + 1], axis=1, keepdims=True)
        output = jnp.where(row >= t, output + shown * now, output)
    delta = jnp.where(row < width, delta, 0.0)
    turn = (((0,), (0,)), ((), ()))
    key_pair, delta_pair = pair(key), pair(delta)
    both = lax.dot_general(key_pair, delta_pair, turn, preferred_element_type=F32)
    both = both[:depth] + both[depth:]
    memory = pair(memory + both[:, :depth] + both[:, depth:])
    opened_ref[...] = output
    gain = small_ref[3 * (width + 1) : 3 * (width + 1) + 1, :]
    for c in range(local_ref.shape[0]):
        output = local_ref[c] + product(carry_ref[c], memory)
        if c == 0:
            tall = lax.broadcasted_iota(jnp.int32, output.shape, 0)
            opened = jnp.concatenate([opened_ref[...], jnp.zeros_like(output[8:])], axis=0)
            output = jnp.where((tall < width) & later, opened, output)
        scale = lax.rsqrt(jnp.mean(output * output, axis=-1, keepdims=True) + 1e-05)
        out_ref[c] = (output * scale * gain).astype(BF16)


def unpack_kernel(piece_ref, out_ref):
    depth = piece_ref.shape[2]
    for head in range(piece_ref.shape[0]):
        out_ref[:, head * depth : (head + 1) * depth] = piece_ref[head]


def compose(later, earlier):
    join = functools.partial(jnp.einsum, "ij,jk->ik", precision=lax.Precision.HIGHEST)
    return jnp.stack([join(later[0], earlier[0]), join(later[0], earlier[1]) + later[1]])


def opening_map(width, taps, tails, first):
    made = []
    for index in range(1, 3):
        rows = jnp.concatenate(
            [tails[width * index : width * (index + 1)], first[8 * index - 8 : 8 * index - 8 + width]]
        )
        own = taken(index, taps, width)
        total = sum(rows[tap : tap + width] * own[tap] for tap in range(width + 1))
        made.append(total / (1.0 + jnp.exp(-total)))
    keys = unit(made[0])
    rates = first[16]
    depth = keys.shape[1]
    maps = jnp.stack([jnp.eye(depth, dtype=F32), jnp.zeros((depth, depth), F32)])
    for t in range(width):
        outer = rates[t] * keys[t][:, None]
        one = jnp.stack([jnp.eye(depth, dtype=F32) - outer * keys[t], outer * made[1][t]])
        maps = compose(one, maps)
    return maps


WHOLE = pl.BlockSpec(memory_space=pltpu.VMEM)
ANY = pl.BlockSpec(memory_space=pl.ANY)


def call(kernel, specs, args, outs, scratch=(), limit=VMEM_LIMIT, out_spec=WHOLE):
    shapes = [jax.ShapeDtypeStruct(shape, dtype) for shape, dtype in outs]
    single = len(shapes) == 1
    return pl.pallas_call(
        kernel,
        out_shape=shapes[0] if single else shapes,
        in_specs=specs,
        out_specs=out_spec if single else [out_spec] * len(shapes),
        scratch_shapes=scratch,
        compiler_params=pltpu.CompilerParams(vmem_limit_bytes=limit),
    )(*args)


def shards(queries, key_rows, value_rows, strength, conv_weight, out_gain):
    taps = conv_weight.shape[1]
    width = taps - 1
    span, heads = strength.shape
    depth = queries.shape[1] // heads
    count = lax.axis_size("seq")
    place = lax.axis_index("seq")
    blocks = count // heads
    assert blocks * heads == count and span == depth and heads & (heads - 1) == 0
    groups = [[b * heads + h for h in range(heads)] for b in range(blocks)]
    block = place // heads

    def share(x):
        return lax.all_to_all(x, "seq", 0, 0, axis_index_groups=groups, tiled=True)

    rows = pltpu.VMEM((span, heads * depth), BF16)
    small = ((16, depth), F32)
    assert 3 * taps < small[0][0] and 3 + width <= EXTRA and 3 * width <= 16
    packed = call(
        functools.partial(pack_kernel, width),
        [ANY] * 6,
        (queries, key_rows, value_rows, strength.T, conv_weight, out_gain.reshape(1, depth)),
        [((heads, 2 * span + EXTRA, depth), BF16)] + [((span, depth), BF16)] * heads + [small],
        [rows] * 3
        + [pltpu.VMEM((heads, span), F32), pltpu.VMEM(conv_weight.shape, BF16), pltpu.VMEM((1, depth), F32)]
        + [pltpu.VMEM((heads, EXTRA, depth), F32), pltpu.VMEM((heads, EXTRA, depth), BF16), pltpu.VMEM(*small)]
        + [pltpu.SemaphoreType.DMA((6,)), pltpu.SemaphoreType.DMA((3 * heads + 2,))],
        limit=VMEM_PACK,
        out_spec=ANY,
    )
    small = packed[-1]
    raw = share(packed[0])
    pieces = {0: packed[1]}
    for slot in sorted(range(1, heads), key=lambda d: (-(d // 2), d)):
        pairs = [(i, i ^ slot) for i in range(count)]
        pieces[slot] = lax.ppermute(packed[1 + slot], "seq", pairs)
    pieces = [pieces[slot] for slot in range(heads)]
    ext = [pltpu.VMEM((heads * span + 8, depth), F32)]
    pairs = ((heads, span, 2 * depth), BF16)
    square = (depth, 2 * depth)
    key, mix, show, factor, opener = call(
        functools.partial(keys_kernel, width),
        [WHOLE] * 2,
        (small, raw),
        [pairs] * 3 + [((len(scan_index(heads)), *square), BF16), (square, BF16)],
        ext + [pltpu.VMEM((heads, *square), BF16)],
    )
    value, memories, final, first = call(
        functools.partial(values_kernel, width),
        [WHOLE] * 4,
        (small, raw, show, factor),
        [pairs, ((heads - 1, *square), BF16), ((depth + 16, depth), F32), ((24, depth), F32)],
        ext,
    )
    ring = [(i, (i + heads) % count) for i in range(count)]
    memory = lax.ppermute(final, "seq", ring)
    if blocks > 2:
        tails = memory[depth:]
        start = jnp.stack([jnp.eye(depth, dtype=F32), jnp.zeros((depth, depth), F32)])

        def joined(x):
            return x[:, :depth].astype(F32) + x[:, depth:].astype(F32)

        join = functools.partial(jnp.matmul, precision=lax.Precision.HIGHEST)
        whole = prefixes(heads, joined(opener), lambda at: joined(factor[at]), join)[-1]
        opened = jnp.where(block > 0, opening_map(width, small, tails, first), start)
        arrived = lax.ppermute(compose(jnp.stack([whole, final[:depth]]), opened), "seq", ring)
        prefix = jnp.where(block > 0, arrived, start)
        reach = 1
        while reach < blocks - 1:
            shift = [(i, (i + reach * heads) % count) for i in range(count)]
            arrived = lax.ppermute(prefix, "seq", shift)
            prefix = jnp.where(block >= reach, compose(prefix, arrived), prefix)
            reach *= 2
        memory = jnp.concatenate([prefix[1], tails])
    local, carry, start_rows = call(
        functools.partial(queries_kernel, width),
        [WHOLE] * (7 + heads),
        (small, key, mix, value, opener, factor, memories, *pieces),
        [((heads, span, depth), F32), pairs, ((8, depth), F32)],
        ext,
    )
    mixed = call(
        functools.partial(finish_kernel, width),
        [WHOLE] * 6,
        (small, start_rows, first, local, carry, memory),
        [((heads, span, depth), BF16)],
        [pltpu.VMEM((3, 16, depth), F32), pltpu.VMEM((8, depth), F32)],
    )
    return call(unpack_kernel, [WHOLE], (share(mixed),), [((span, heads * depth), BF16)])


def solution(mesh):
    placed = (
        P(("groups", "seq"), None),
        P(("groups", "seq"), None),
        P(("groups", "seq"), None),
        P(("groups", "seq"), None),
        P(),
        P(),
    )
    return jax.shard_map(
        shards, mesh=mesh, in_specs=placed, out_specs=P(("groups", "seq"), None), check_vma=False
    )
```

```python
import functools

import jax
import jax.numpy as jnp
from jax import lax
from jax.experimental import pallas as pl
from jax.experimental.pallas import tpu as pltpu
from jax.sharding import PartitionSpec as P


EXTRA = 8
FOLD = 32
VMEM_LIMIT = 24 * 1024 * 1024
VMEM_PACK = 66200000
F32 = jnp.float32
BF16 = jnp.bfloat16


def pair(x):
    high = x.astype(BF16)
    return jnp.concatenate([high, (x - high.astype(F32)).astype(BF16)], axis=1)


def product(lhs, rhs):
    both = jnp.dot(lhs, jnp.concatenate([rhs, rhs], axis=0), preferred_element_type=F32)
    half = both.shape[1] // 2
    return both[:, :half] + both[:, half:]


def product_t(lhs, rhs):
    k = rhs.shape[1] // 2
    high, low = rhs[:, :k], rhs[:, k:]
    rhs = jnp.concatenate(
        [jnp.concatenate([high, high], axis=1), jnp.concatenate([low, low], axis=1)], axis=0
    )
    both = lax.dot_general(lhs, rhs, (((1,), (1,)), ((), ())), preferred_element_type=F32)
    half = both.shape[1] // 2
    return both[:, :half] + both[:, half:]


def position(heads):
    place = lax.axis_index("seq")
    return lax.rem(place, heads), lax.div(place, heads)


def pack_kernel(q_hbm, k_hbm, v_hbm, rate_hbm, taps_hbm, gain_hbm, keys_hbm, *refs):
    pieces, small_hbm = refs[:-12], refs[-12]
    q_ref, k_ref, v_ref, rate_ref, taps_ref, gain_ref, parts_ref, extra_ref, small_ref, in_sems, out_sems = refs[-11:]
    heads, span = rate_ref.shape
    depth = q_ref.shape[1] // heads
    own = position(heads)[0]
    arrivals = (
        (rate_hbm, rate_ref),
        (k_hbm, k_ref),
        (v_hbm, v_ref),
        (q_hbm, q_ref),
        (taps_hbm, taps_ref),
        (gain_hbm, gain_ref),
    )
    arriving = [pltpu.make_async_copy(*ends, in_sems.at[index]) for index, ends in enumerate(arrivals)]
    for copy in arriving:
        copy.start()
    leaving = []

    def leave(source, target):
        leaving.append(pltpu.make_async_copy(source, target, out_sems.at[len(leaving)]))
        leaving[-1].start()

    parts_ref[...] = jnp.zeros_like(parts_ref)
    arriving[0].wait()
    rate = rate_ref[...]
    for part in range(3):
        high = rate.astype(BF16).astype(F32)
        for head in range(heads):
            parts_ref[head, part : part + 1, :] = high[head : head + 1]
        rate = rate - high
    extra_ref[...] = parts_ref[...].astype(BF16)
    arriving[1].wait()
    for head in range(heads):
        leave(k_ref.at[:, head * depth : (head + 1) * depth], keys_hbm.at[head, :span, :])
    leave(extra_ref, keys_hbm.at[:, span:, :])
    own_lanes = pl.ds(pl.multiple_of(own * depth, depth), depth)
    for index, source in enumerate((v_ref, q_ref)):
        arriving[2 + index].wait()
        for slot in range(heads):
            lanes = pl.ds(pl.multiple_of((own ^ slot) * depth, depth), depth)
            leave(source.at[:, lanes], pieces[slot].at[index * span : (index + 1) * span, :])
    arriving[4].wait()
    arriving[5].wait()
    count = taps_ref.shape[1]
    for index in range(3):
        small_ref[index * count : (index + 1) * count, :] = taps_ref[index, :, own_lanes].astype(F32)
    small_ref[3 * count : 3 * count + 1, :] = gain_ref[...]
    leave(small_ref, small_hbm)
    for copy in leaving:
        copy.wait()


def convolved(ext_ref, first, rows, taps):
    total = ext_ref[first : first + rows, :] * taps[:1]
    for tap in range(1, taps.shape[0]):
        total += ext_ref[first + tap : first + tap + rows, :] * taps[tap : tap + 1]
    return total / (1.0 + jnp.exp(-total))


def stage_keys(raw_ref, ext_ref):
    span = raw_ref.shape[1] - EXTRA
    ext_ref[:8, :] = jnp.zeros_like(ext_ref[:8, :])
    for c in range(raw_ref.shape[0]):
        ext_ref[8 + c * span : 8 + (c + 1) * span, :] = raw_ref[c, :span, :].astype(F32)


def stage(pieces, index, ext_ref):
    span = pieces[0].shape[0] // 2
    ext_ref[:8, :] = jnp.zeros_like(ext_ref[:8, :])
    for slot, piece in enumerate(pieces):
        rows = pl.ds(pl.multiple_of(8 + (position(len(pieces))[0] ^ slot) * span, 8), span)
        ext_ref[rows, :] = piece[index * span : (index + 1) * span, :].astype(F32)


def taken(index, taps, width):
    return taps[index * (width + 1) : (index + 1) * (width + 1)]


def rate_row(raw_ref, c):
    parts = raw_ref[c, raw_ref.shape[1] - EXTRA :, :].astype(F32)
    return parts[:1] + parts[1:2] + parts[2:3]


def unit(x):
    return x * lax.rsqrt(jnp.sum(x * x, axis=-1, keepdims=True) + 1e-06)


def grids(span):
    row = lax.broadcasted_iota(jnp.int32, (span, span), 0)
    col = lax.broadcasted_iota(jnp.int32, (span, span), 1)
    return row, col, (row == col).astype(F32)


def scan_plan(chunks):
    plan, reach = [], 1
    while reach < chunks:
        plan.append([(c, (c // reach) * reach - 1) for c in range(chunks) if c // reach % 2])
        reach *= 2
    return plan


def scan_updates(chunks):
    wanted, updates = set(), []
    for level in reversed(scan_plan(chunks)):
        grown = [(c, earlier) for c, earlier in level if c in wanted]
        updates.append({c for c, _ in grown})
        wanted |= {c for c, _ in level} | {earlier for _, earlier in grown}
    return updates[::-1]


def scan_index(chunks):
    return {pair_: at for at, pair_ in enumerate(p for level in scan_plan(chunks) for p in level)}


def prefixes(chunks, first, factor, join):
    maps, index = [first], scan_index(1 << (chunks - 1).bit_length())
    for c in range(1, chunks):
        earlier = (1 << (c.bit_length() - 1)) - 1
        maps.append(join(factor(index[c, earlier]), maps[earlier]))
    return maps


def fold_product(lhs, rhs, width):
    lanes = rhs.shape[1]
    if width == lanes:
        return product(lhs, pair(rhs))
    at = lax.broadcasted_iota(jnp.int32, rhs.shape, 1) // width
    high = rhs.astype(BF16).astype(F32)
    parts = (high, rhs - high)
    rows = [
        jnp.concatenate([jnp.where(at == i, part, 0.0).astype(BF16) for part in parts], axis=1)
        for i in range(lanes // width)
    ]
    both = jnp.dot(lhs, jnp.concatenate(rows + rows, axis=0), preferred_element_type=F32)
    return both[:, :lanes] + both[:, lanes:]


def inverse_of(lowers):
    span = lowers[0].shape[0]
    width = FOLD
    lane = lax.broadcasted_iota(jnp.int32, (width, span), 1)
    inner = lowers
    while inner[0].shape[0] > width:
        half = inner[0].shape[0] // 2
        side = lax.broadcasted_iota(jnp.int32, (half, span), 1) // half % 2
        inner = [jnp.where(side == 0, x[:half], x[half:]) for x in inner]
    row = lax.broadcasted_iota(jnp.int32, (width, span), 0)
    col = lane % width
    done = [(row == col).astype(F32) - jnp.where((row ^ col) == 1, x, 0.0) for x in inner]
    size = 2
    while size < span:
        wide = min(4 * size, span)
        if wide > width:
            side = lax.broadcasted_iota(jnp.int32, (width, span), 1) // width
            done = [
                jnp.concatenate([jnp.where(side == i, x, 0.0) for i in range(span // width)], axis=0) for x in done
            ]
            width, inner = span, lowers
            row = lax.broadcasted_iota(jnp.int32, (width, span), 0)
            col = lax.broadcasted_iota(jnp.int32, (width, span), 1)
        pick = (row // wide == col // wide) & (row // size != col // size)
        pairs = [pair(x) for x in done]
        z = [fold_product(y, jnp.where(pick, x, 0.0), width) for x, y in zip(inner, pairs)]
        pairs = [pair(x) for x in z]
        square = [fold_product(y, x, width) for x, y in zip(z, pairs)]
        done = [x - fold_product(y, x, width) for x, y in zip(done, pairs)]
        done = [x + fold_product(pair(y), x, width) for x, y in zip(done, square)]
        size = wide
    return done


def keys_kernel(width, small_ref, raw_ref, key_ref, mix_ref, show_ref, factor_ref, open_ref, ext_ref, run_ref):
    chunks = raw_ref.shape[0]
    span = raw_ref.shape[1] - EXTRA
    row, col, eye = grids(span)
    taps = taken(1, small_ref[...], width)
    stage_keys(raw_ref, ext_ref)
    lowers, rates, turned = [], [], []
    for c in range(chunks):
        key = unit(convolved(ext_ref, 8 - width + c * span, span, taps))
        rates.append(rate_row(raw_ref, c))
        if c == 0:
            rates[c] = jnp.where((col[:1] < width) & (position(chunks)[1] > 0), 0.0, rates[c])
        rate = jnp.sum(eye * rates[c], axis=1, keepdims=True)
        key_pair = pair(key)
        key_ref[c] = key_pair
        turned.append(pair(key.T))
        lowers.append(jnp.where(row > col, rate * product_t(key_pair, key_pair), 0.0))
    inverses = inverse_of(lowers)
    for c in range(chunks):
        mix = pair(inverses[c] * rates[c])
        mix_ref[c] = mix
        show = pair(product(turned[c], mix))
        show_ref[c] = show
        run_ref[c] = pair(eye - product(show, key_ref[c]))
    open_ref[...] = run_ref[0]
    at = 0
    for level, grown in zip(scan_plan(chunks), scan_updates(chunks)):
        for c, earlier in level:
            factor_ref[at] = run_ref[c]
            at += 1
        for c, earlier in level:
            if c in grown:
                run_ref[c] = pair(product(run_ref[c], run_ref[earlier]))


def values_of(width, small_ref, pieces, ext_ref):
    span = pieces[0].shape[0] // 2
    taps = taken(2, small_ref[...], width)
    stage(pieces, 0, ext_ref)
    return [pair(convolved(ext_ref, 8 - width + c * span, span, taps)) for c in range(len(pieces))]


def states_of(show_ref, factor_ref, values):
    states = [product(show_ref[c], value) for c, value in enumerate(values)]
    at = 0
    for level in scan_plan(len(values)):
        for c, earlier in level:
            states[c] = states[c] + product(factor_ref[at], pair(states[earlier]))
            at += 1
    return states


def state_kernel(width, last, small_ref, raw_ref, show_ref, factor_ref, *refs):
    pieces, (final_ref, ext_ref, edge_ref) = refs[:-3], refs[-3:]
    chunks, depth = raw_ref.shape[0], raw_ref.shape[2]
    span = raw_ref.shape[1] - EXTRA
    read = position(chunks)[1] < last

    @pl.when(jnp.logical_not(read))
    def _():
        final_ref[...] = jnp.zeros_like(final_ref)

    @pl.when(read)
    def _():
        values = values_of(width, small_ref, pieces, ext_ref)
        final_ref[:depth, :] = states_of(show_ref, factor_ref, values)[-1]
        for slot, piece in enumerate(pieces):
            chunk = position(chunks)[0] ^ slot
            edge_ref[pl.ds(pl.multiple_of(8 * chunk, 8), 8), :] = piece[2 * span - 8 :, :].astype(F32)
        final_ref[depth : depth + width, :] = edge_ref[8 * chunks - width : 8 * chunks, :]
        keys = raw_ref[chunks - 1, span - width : span, :]
        final_ref[depth + width : depth + 2 * width, :] = keys.astype(F32)
        end = 8 + chunks * span
        final_ref[depth + 2 * width : depth + 3 * width, :] = ext_ref[end - width : end, :]
        final_ref[depth + 3 * width :, :] = jnp.zeros_like(final_ref[depth + 3 * width :, :])


def queries_kernel(width, small_ref, raw_ref, key_ref, mix_ref, show_ref, open_ref, factor_ref, *refs):
    pieces, (local_ref, carry_ref, first_ref, values_ext, ext_ref) = refs[:-5], refs[-5:]
    chunks, span = key_ref.shape[0], key_ref.shape[1]
    row, col, _ = grids(span)
    values = values_of(width, small_ref, pieces, values_ext)
    states = states_of(show_ref, factor_ref, values)
    taps = taken(0, small_ref[...], width)
    stage(pieces, 1, ext_ref)
    first_ref[:8, :] = ext_ref[8:16, :]
    first_ref[8:16, :] = raw_ref[0, :8, :].astype(F32)
    first_ref[16:24, :] = values_ext[8:16, :]
    first_ref[24:25, :] = rate_row(raw_ref, 0)
    queries = [unit(convolved(ext_ref, 8 - width + c * span, span, taps)) for c in range(chunks)]
    mixed = [
        pair(jnp.where(row >= col, product_t(pair(queries[c]), key_ref[c]), 0.0)) for c in range(chunks)
    ]
    mixed = [pair(product(mixed[c], mix_ref[c])) for c in range(chunks)]
    seen = [pair(queries[c] - product(mixed[c], key_ref[c])) for c in range(chunks)]
    local = [product(mixed[c], values[c]) for c in range(chunks)]
    local_ref[0] = local[0]
    carry_ref[0] = seen[0]
    through = prefixes(
        chunks - 1, open_ref[...], lambda at: factor_ref[at], lambda x, y: pair(product(x, y))
    )
    for c in range(1, chunks):
        local_ref[c] = local[c] + product(seen[c], pair(states[c - 1]))
        carry_ref[c] = pair(product(seen[c], through[c - 1]))


def opening(width, taps, tails, start_ref, ext_ref):
    made = []
    for index in range(3):
        ext_ref[index, 8 - width : 8, :] = tails[width * index : width * (index + 1)]
        ext_ref[index, 8:, :] = start_ref[8 * index : 8 * index + 8, :]
        made.append(convolved(ext_ref.at[index], 8 - width, 8, taken(index, taps, width)))
    rates = start_ref[24:25, :]
    row = lax.broadcasted_iota(jnp.int32, (8, rates.shape[1]), 0)
    col = lax.broadcasted_iota(jnp.int32, (8, rates.shape[1]), 1)
    strengths = jnp.sum(jnp.where((row == col) & (row < width), rates, 0.0), axis=1, keepdims=True)
    return unit(made[0]), unit(made[1]), made[2], strengths


def finish_kernel(width, small_ref, start_ref, local_ref, carry_ref, memory_ref, *refs):
    outs, (ext_ref, first_ref) = refs[:-2], refs[-2:]
    depth = local_ref.shape[2]
    later = position(local_ref.shape[0])[1] > 0
    memory = jnp.where(later, memory_ref[:depth, :], 0.0)
    tails = jnp.where(later, memory_ref[depth:, :], 0.0)
    taps = small_ref[...]
    query, key, value, rate = opening(width, taps, tails, start_ref, ext_ref)
    rate = jnp.where(later, rate, 0.0)
    seen = product(pair(jnp.concatenate([key, query], axis=0)), pair(memory))
    delta = rate * (value - seen[:8])
    row = lax.broadcasted_iota(jnp.int32, delta.shape, 0)
    output = seen[8:]
    for t in range(width):
        now = delta[t : t + 1]
        meets = jnp.sum(key * key[t : t + 1], axis=1, keepdims=True)
        delta = jnp.where(row > t, delta - rate * meets * now, delta)
        shown = jnp.sum(query * key[t : t + 1], axis=1, keepdims=True)
        output = jnp.where(row >= t, output + shown * now, output)
    delta = jnp.where(row < width, delta, 0.0)
    turn = (((0,), (0,)), ((), ()))
    key_pair, delta_pair = pair(key), pair(delta)
    both = lax.dot_general(key_pair, delta_pair, turn, preferred_element_type=F32)
    both = both[:depth] + both[depth:]
    memory = pair(memory + both[:, :depth] + both[:, depth:])
    first_ref[...] = output
    gain = small_ref[3 * (width + 1) : 3 * (width + 1) + 1, :]
    own = position(local_ref.shape[0])[0]
    opened = jnp.concatenate([first_ref[...], jnp.zeros_like(local_ref[0, 8:, :])], axis=0)
    tall = lax.broadcasted_iota(jnp.int32, opened.shape, 0)
    for slot, out_ref in enumerate(outs):
        c = own ^ slot
        output = local_ref[c] + product(carry_ref[c], memory)
        output = jnp.where((tall < width) & later & (c == 0), opened, output)
        scale = lax.rsqrt(jnp.mean(output * output, axis=-1, keepdims=True) + 1e-05)
        out_ref[...] = (output * scale * gain).astype(BF16)


def unpack_kernel(*refs):
    pieces, out_ref = refs[:-1], refs[-1]
    depth = pieces[0].shape[1]
    own = position(len(pieces))[0]
    for slot, piece in enumerate(pieces):
        lanes = pl.ds(pl.multiple_of((own ^ slot) * depth, depth), depth)
        out_ref[:, lanes] = piece[...]


def compose(later, earlier):
    join = functools.partial(jnp.einsum, "ij,jk->ik", precision=lax.Precision.HIGHEST)
    return jnp.stack([join(later[0], earlier[0]), join(later[0], earlier[1]) + later[1]])


def opening_map(width, taps, tails, first):
    made = []
    for index in range(1, 3):
        rows = jnp.concatenate(
            [tails[width * index : width * (index + 1)], first[8 * index : 8 * index + width]]
        )
        own = taken(index, taps, width)
        total = sum(rows[tap : tap + width] * own[tap] for tap in range(width + 1))
        made.append(total / (1.0 + jnp.exp(-total)))
    keys = unit(made[0])
    rates = first[24]
    depth = keys.shape[1]
    maps = jnp.stack([jnp.eye(depth, dtype=F32), jnp.zeros((depth, depth), F32)])
    for t in range(width):
        outer = rates[t] * keys[t][:, None]
        one = jnp.stack([jnp.eye(depth, dtype=F32) - outer * keys[t], outer * made[1][t]])
        maps = compose(one, maps)
    return maps


WHOLE = pl.BlockSpec(memory_space=pltpu.VMEM)
ANY = pl.BlockSpec(memory_space=pl.ANY)


def call(kernel, specs, args, outs, scratch=(), limit=VMEM_LIMIT, out_spec=WHOLE):
    shapes = [jax.ShapeDtypeStruct(shape, dtype) for shape, dtype in outs]
    single = len(shapes) == 1
    return pl.pallas_call(
        kernel,
        out_shape=shapes[0] if single else shapes,
        in_specs=specs,
        out_specs=out_spec if single else [out_spec] * len(shapes),
        scratch_shapes=scratch,
        compiler_params=pltpu.CompilerParams(vmem_limit_bytes=limit),
    )(*args)


def exchange(pieces, count):
    arrived = [pieces[0]]
    for slot in range(1, len(pieces)):
        pairs = [(i, i ^ slot) for i in range(count)]
        arrived.append(lax.ppermute(pieces[slot], "seq", pairs))
    return arrived


def shards(queries, key_rows, value_rows, strength, conv_weight, out_gain):
    taps = conv_weight.shape[1]
    width = taps - 1
    span, heads = strength.shape
    depth = queries.shape[1] // heads
    count = lax.axis_size("seq")
    place = lax.axis_index("seq")
    blocks = count // heads
    assert blocks * heads == count and span == depth and heads & (heads - 1) == 0
    groups = [[b * heads + h for h in range(heads)] for b in range(blocks)]
    block = place // heads

    def share(x):
        return lax.all_to_all(x, "seq", 0, 0, axis_index_groups=groups, tiled=True)

    rows = pltpu.VMEM((span, heads * depth), BF16)
    small = ((16, depth), F32)
    assert 3 * taps < small[0][0]
    packed = call(
        pack_kernel,
        [ANY] * 6,
        (queries, key_rows, value_rows, strength.T, conv_weight, out_gain.reshape(1, depth)),
        [((heads, span + EXTRA, depth), BF16)] + [((2 * span, depth), BF16)] * heads + [small],
        [rows] * 3
        + [pltpu.VMEM((heads, span), F32), pltpu.VMEM(conv_weight.shape, BF16), pltpu.VMEM((1, depth), F32)]
        + [pltpu.VMEM((heads, EXTRA, depth), F32), pltpu.VMEM((heads, EXTRA, depth), BF16), pltpu.VMEM(*small)]
        + [pltpu.SemaphoreType.DMA((6,)), pltpu.SemaphoreType.DMA((3 * heads + 2,))],
        limit=VMEM_PACK,
        out_spec=ANY,
    )
    small = packed[-1]
    raw = share(packed[0])
    pieces = exchange(packed[1 : 1 + heads], count)
    ext = [pltpu.VMEM((heads * span + 8, depth), F32)]
    pairs = ((heads, span, 2 * depth), BF16)
    square = (depth, 2 * depth)
    key, mix, show, factor, opener = call(
        functools.partial(keys_kernel, width),
        [WHOLE] * 2,
        (small, raw),
        [pairs] * 3 + [((len(scan_index(heads)), *square), BF16), (square, BF16)],
        ext + [pltpu.VMEM((heads, *square), BF16)],
    )
    final = call(
        functools.partial(state_kernel, width, blocks - 1),
        [WHOLE] * (4 + heads),
        (small, raw, show, factor, *pieces),
        [((depth + 16, depth), F32)],
        ext + [pltpu.VMEM((8 * heads, depth), F32)],
    )
    ring = [(i, (i + heads) % count) for i in range(count)]
    memory = lax.ppermute(final, "seq", ring)
    local, carry, first = call(
        functools.partial(queries_kernel, width),
        [WHOLE] * (7 + heads),
        (small, raw, key, mix, show, opener, factor, *pieces),
        [((heads, span, depth), F32), pairs, ((32, depth), F32)],
        ext * 2,
    )
    if blocks > 2:
        tails = memory[depth:]
        start = jnp.stack([jnp.eye(depth, dtype=F32), jnp.zeros((depth, depth), F32)])

        def joined(x):
            return x[:, :depth].astype(F32) + x[:, depth:].astype(F32)

        join = functools.partial(jnp.matmul, precision=lax.Precision.HIGHEST)
        whole = prefixes(heads, joined(opener), lambda at: joined(factor[at]), join)[-1]
        opened = jnp.where(block > 0, opening_map(width, small, tails, first), start)
        arrived = lax.ppermute(compose(jnp.stack([whole, final[:depth]]), opened), "seq", ring)
        prefix = jnp.where(block > 0, arrived, start)
        reach = 1
        while reach < blocks - 1:
            shift = [(i, (i + reach * heads) % count) for i in range(count)]
            arrived = lax.ppermute(prefix, "seq", shift)
            prefix = jnp.where(block >= reach, compose(prefix, arrived), prefix)
            reach *= 2
        memory = jnp.concatenate([prefix[1], tails])
    mixed = call(
        functools.partial(finish_kernel, width),
        [WHOLE] * 5,
        (small, first, local, carry, memory),
        [((span, depth), BF16)] * heads,
        [pltpu.VMEM((3, 16, depth), F32), pltpu.VMEM((8, depth), F32)],
    )
    mixed = exchange(mixed, count)
    return call(unpack_kernel, [WHOLE] * heads, mixed, [((span, heads * depth), BF16)])


def solution(mesh):
    placed = (
        P(("groups", "seq"), None),
        P(("groups", "seq"), None),
        P(("groups", "seq"), None),
        P(("groups", "seq"), None),
        P(),
        P(),
    )
    return jax.shard_map(
        shards, mesh=mesh, in_specs=placed, out_specs=P(("groups", "seq"), None), check_vma=False
    )
```

```python
import functools

import jax
import jax.numpy as jnp
from jax import lax
from jax.experimental import pallas as pl
from jax.experimental.pallas import tpu as pltpu
from jax.sharding import PartitionSpec as P


EXTRA = 8
FOLD = 32
VMEM_LIMIT = 24 * 1024 * 1024
VMEM_PACK = 66200000
F32 = jnp.float32
BF16 = jnp.bfloat16


def pair(x):
    high = x.astype(BF16)
    return jnp.concatenate([high, (x - high.astype(F32)).astype(BF16)], axis=1)


def product(lhs, rhs):
    both = jnp.dot(lhs, jnp.concatenate([rhs, rhs], axis=0), preferred_element_type=F32)
    half = both.shape[1] // 2
    return both[:, :half] + both[:, half:]


def product_t(lhs, rhs):
    k = rhs.shape[1] // 2
    high, low = rhs[:, :k], rhs[:, k:]
    rhs = jnp.concatenate(
        [jnp.concatenate([high, high], axis=1), jnp.concatenate([low, low], axis=1)], axis=0
    )
    both = lax.dot_general(lhs, rhs, (((1,), (1,)), ((), ())), preferred_element_type=F32)
    half = both.shape[1] // 2
    return both[:, :half] + both[:, half:]


def position(heads):
    place = lax.axis_index("seq")
    return lax.rem(place, heads), lax.div(place, heads)


def pack_kernel(q_hbm, k_hbm, v_hbm, rate_hbm, taps_hbm, gain_hbm, *refs):
    outs, small_hbm = refs[:-12], refs[-12]
    keys, pieces = outs[: len(outs) // 2], outs[len(outs) // 2 :]
    q_ref, k_ref, v_ref, rate_ref, taps_ref, gain_ref, parts_ref, extra_ref, small_ref, in_sems, out_sems = refs[-11:]
    heads, span = rate_ref.shape
    depth = q_ref.shape[1] // heads
    own = position(heads)[0]
    arrivals = (
        (rate_hbm, rate_ref),
        (k_hbm, k_ref),
        (v_hbm, v_ref),
        (q_hbm, q_ref),
        (taps_hbm, taps_ref),
        (gain_hbm, gain_ref),
    )
    arriving = [pltpu.make_async_copy(*ends, in_sems.at[index]) for index, ends in enumerate(arrivals)]
    for copy in arriving:
        copy.start()
    leaving = []

    def leave(source, target):
        leaving.append(pltpu.make_async_copy(source, target, out_sems.at[len(leaving)]))
        leaving[-1].start()

    parts_ref[...] = jnp.zeros_like(parts_ref)
    arriving[0].wait()
    rate = rate_ref[...]
    for part in range(3):
        high = rate.astype(BF16).astype(F32)
        for head in range(heads):
            parts_ref[head, part : part + 1, :] = high[head : head + 1]
        rate = rate - high
    extra_ref[...] = parts_ref[...].astype(BF16)
    own_lanes = pl.ds(pl.multiple_of(own * depth, depth), depth)
    arriving[1].wait()
    for slot in range(heads):
        lanes = pl.ds(pl.multiple_of((own ^ slot) * depth, depth), depth)
        leave(extra_ref.at[own ^ slot], keys[slot].at[span:, :])
        leave(k_ref.at[:, lanes], keys[slot].at[:span, :])
    for index, source in enumerate((v_ref, q_ref)):
        arriving[2 + index].wait()
        for slot in range(heads):
            lanes = pl.ds(pl.multiple_of((own ^ slot) * depth, depth), depth)
            leave(source.at[:, lanes], pieces[slot].at[index * span : (index + 1) * span, :])
    arriving[4].wait()
    arriving[5].wait()
    count = taps_ref.shape[1]
    for index in range(3):
        small_ref[index * count : (index + 1) * count, :] = taps_ref[index, :, own_lanes].astype(F32)
    small_ref[3 * count : 3 * count + 1, :] = gain_ref[...]
    leave(small_ref, small_hbm)
    for copy in leaving:
        copy.wait()


def convolved(ext_ref, first, rows, taps):
    total = ext_ref[first : first + rows, :] * taps[:1]
    for tap in range(1, taps.shape[0]):
        total += ext_ref[first + tap : first + tap + rows, :] * taps[tap : tap + 1]
    return total / (1.0 + jnp.exp(-total))


def stage(pieces, index, span, ext_ref):
    ext_ref[:8, :] = jnp.zeros_like(ext_ref[:8, :])
    for slot, piece in enumerate(pieces):
        rows = pl.ds(pl.multiple_of(8 + (position(len(pieces))[0] ^ slot) * span, 8), span)
        ext_ref[rows, :] = piece[index * span : (index + 1) * span, :].astype(F32)


def taken(index, taps, width):
    return taps[index * (width + 1) : (index + 1) * (width + 1)]


def unit(x):
    return x * lax.rsqrt(jnp.sum(x * x, axis=-1, keepdims=True) + 1e-06)


def grids(span):
    row = lax.broadcasted_iota(jnp.int32, (span, span), 0)
    col = lax.broadcasted_iota(jnp.int32, (span, span), 1)
    return row, col, (row == col).astype(F32)


def scan_plan(chunks):
    plan, reach = [], 1
    while reach < chunks:
        plan.append([(c, (c // reach) * reach - 1) for c in range(chunks) if c // reach % 2])
        reach *= 2
    return plan


def scan_updates(chunks):
    wanted, updates = set(), []
    for level in reversed(scan_plan(chunks)):
        grown = [(c, earlier) for c, earlier in level if c in wanted]
        updates.append({c for c, _ in grown})
        wanted |= {c for c, _ in level} | {earlier for _, earlier in grown}
    return updates[::-1]


def scan_index(chunks):
    return {pair_: at for at, pair_ in enumerate(p for level in scan_plan(chunks) for p in level)}


def prefixes(chunks, first, factor, join):
    maps, index = [first], scan_index(1 << (chunks - 1).bit_length())
    for c in range(1, chunks):
        earlier = (1 << (c.bit_length() - 1)) - 1
        maps.append(join(factor(index[c, earlier]), maps[earlier]))
    return maps


def fold_product(lhs, rhs, width):
    lanes = rhs.shape[1]
    if width == lanes:
        return product(lhs, pair(rhs))
    at = lax.broadcasted_iota(jnp.int32, rhs.shape, 1) // width
    high = rhs.astype(BF16).astype(F32)
    parts = (high, rhs - high)
    rows = [
        jnp.concatenate([jnp.where(at == i, part, 0.0).astype(BF16) for part in parts], axis=1)
        for i in range(lanes // width)
    ]
    both = jnp.dot(lhs, jnp.concatenate(rows + rows, axis=0), preferred_element_type=F32)
    return both[:, :lanes] + both[:, lanes:]


def inverse_of(lowers):
    span = lowers[0].shape[0]
    width = FOLD
    lane = lax.broadcasted_iota(jnp.int32, (width, span), 1)
    inner = lowers
    while inner[0].shape[0] > width:
        half = inner[0].shape[0] // 2
        side = lax.broadcasted_iota(jnp.int32, (half, span), 1) // half % 2
        inner = [jnp.where(side == 0, x[:half], x[half:]) for x in inner]
    row = lax.broadcasted_iota(jnp.int32, (width, span), 0)
    col = lane % width
    done = [(row == col).astype(F32) - jnp.where((row ^ col) == 1, x, 0.0) for x in inner]
    size = 2
    while size < span:
        wide = min(4 * size, span)
        if wide > width:
            side = lax.broadcasted_iota(jnp.int32, (width, span), 1) // width
            done = [
                jnp.concatenate([jnp.where(side == i, x, 0.0) for i in range(span // width)], axis=0) for x in done
            ]
            width, inner = span, lowers
            row = lax.broadcasted_iota(jnp.int32, (width, span), 0)
            col = lax.broadcasted_iota(jnp.int32, (width, span), 1)
        pick = (row // wide == col // wide) & (row // size != col // size)
        pairs = [pair(x) for x in done]
        z = [fold_product(y, jnp.where(pick, x, 0.0), width) for x, y in zip(inner, pairs)]
        pairs = [pair(x) for x in z]
        square = [fold_product(y, x, width) for x, y in zip(z, pairs)]
        done = [x - fold_product(y, x, width) for x, y in zip(done, pairs)]
        done = [x + fold_product(pair(y), x, width) for x, y in zip(done, square)]
        size = wide
    return done


def keys_kernel(width, small_ref, *refs):
    pieces = refs[:-9]
    key_ref, mix_ref, show_ref, factor_ref, open_ref, edge_ref, ext_ref, rates_ref, run_ref = refs[-9:]
    chunks = len(pieces)
    span = pieces[0].shape[0] - EXTRA
    row, col, eye = grids(span)
    taps = taken(1, small_ref[...], width)
    stage(pieces, 0, span, ext_ref)
    for slot, piece in enumerate(pieces):
        at = pl.ds(pl.multiple_of((position(chunks)[0] ^ slot) * EXTRA, EXTRA), EXTRA)
        rates_ref[at, :] = piece[span:, :].astype(F32)
    edge_ref[:8, :] = ext_ref[8:16, :]
    edge_ref[8:16, :] = ext_ref[chunks * span : chunks * span + 8, :]
    edge_ref[16:24, :] = jnp.zeros_like(edge_ref[16:24, :])
    edge_ref[16:17, :] = rates_ref[0:1, :] + rates_ref[1:2, :] + rates_ref[2:3, :]
    lowers, rates, turned = [], [], []
    for c in range(chunks):
        key = unit(convolved(ext_ref, 8 - width + c * span, span, taps))
        parts = rates_ref[EXTRA * c : EXTRA * c + EXTRA, :]
        rates.append(parts[:1] + parts[1:2] + parts[2:3])
        if c == 0:
            rates[c] = jnp.where((col[:1] < width) & (position(chunks)[1] > 0), 0.0, rates[c])
        rate = jnp.sum(eye * rates[c], axis=1, keepdims=True)
        key_pair = pair(key)
        key_ref[c] = key_pair
        turned.append(pair(key.T))
        lowers.append(jnp.where(row > col, rate * product_t(key_pair, key_pair), 0.0))
    inverses = inverse_of(lowers)
    for c in range(chunks):
        mix = pair(inverses[c] * rates[c])
        mix_ref[c] = mix
        show = pair(product(turned[c], mix))
        show_ref[c] = show
        run_ref[c] = pair(eye - product(show, key_ref[c]))
    open_ref[...] = run_ref[0]
    at = 0
    for level, grown in zip(scan_plan(chunks), scan_updates(chunks)):
        for c, earlier in level:
            factor_ref[at] = run_ref[c]
            at += 1
        for c, earlier in level:
            if c in grown:
                run_ref[c] = pair(product(run_ref[c], run_ref[earlier]))


def values_of(width, small_ref, pieces, ext_ref):
    span = pieces[0].shape[0] // 2
    taps = taken(2, small_ref[...], width)
    stage(pieces, 0, span, ext_ref)
    return [pair(convolved(ext_ref, 8 - width + c * span, span, taps)) for c in range(len(pieces))]


def states_of(show_ref, factor_ref, values):
    states = [product(show_ref[c], value) for c, value in enumerate(values)]
    at = 0
    for level in scan_plan(len(values)):
        for c, earlier in level:
            states[c] = states[c] + product(factor_ref[at], pair(states[earlier]))
            at += 1
    return states


def state_kernel(width, last, small_ref, keys_ref, show_ref, factor_ref, *refs):
    pieces, (final_ref, ext_ref, edge_ref) = refs[:-3], refs[-3:]
    chunks, span, depth = len(pieces), pieces[0].shape[0] // 2, pieces[0].shape[1]
    read = position(chunks)[1] < last

    @pl.when(jnp.logical_not(read))
    def _():
        final_ref[...] = jnp.zeros_like(final_ref)

    @pl.when(read)
    def _():
        values = values_of(width, small_ref, pieces, ext_ref)
        final_ref[:depth, :] = states_of(show_ref, factor_ref, values)[-1]
        for slot, piece in enumerate(pieces):
            chunk = position(chunks)[0] ^ slot
            edge_ref[pl.ds(pl.multiple_of(8 * chunk, 8), 8), :] = piece[2 * span - 8 :, :].astype(F32)
        final_ref[depth : depth + width, :] = edge_ref[8 * chunks - width : 8 * chunks, :]
        final_ref[depth + width : depth + 2 * width, :] = keys_ref[16 - width : 16, :]
        end = 8 + chunks * span
        final_ref[depth + 2 * width : depth + 3 * width, :] = ext_ref[end - width : end, :]
        final_ref[depth + 3 * width :, :] = jnp.zeros_like(final_ref[depth + 3 * width :, :])


def queries_kernel(width, small_ref, keys_ref, key_ref, mix_ref, show_ref, open_ref, factor_ref, *refs):
    pieces, (local_ref, carry_ref, first_ref, values_ext, ext_ref) = refs[:-5], refs[-5:]
    chunks, span = key_ref.shape[0], key_ref.shape[1]
    row, col, _ = grids(span)
    values = values_of(width, small_ref, pieces, values_ext)
    states = states_of(show_ref, factor_ref, values)
    taps = taken(0, small_ref[...], width)
    stage(pieces, 1, span, ext_ref)
    first_ref[:8, :] = ext_ref[8:16, :]
    first_ref[8:16, :] = keys_ref[:8, :]
    first_ref[16:24, :] = values_ext[8:16, :]
    first_ref[24:32, :] = keys_ref[16:24, :]
    queries = [unit(convolved(ext_ref, 8 - width + c * span, span, taps)) for c in range(chunks)]
    mixed = [
        pair(jnp.where(row >= col, product_t(pair(queries[c]), key_ref[c]), 0.0)) for c in range(chunks)
    ]
    mixed = [pair(product(mixed[c], mix_ref[c])) for c in range(chunks)]
    seen = [pair(queries[c] - product(mixed[c], key_ref[c])) for c in range(chunks)]
    local = [product(mixed[c], values[c]) for c in range(chunks)]
    local_ref[0] = local[0]
    carry_ref[0] = seen[0]
    through = prefixes(
        chunks - 1, open_ref[...], lambda at: factor_ref[at], lambda x, y: pair(product(x, y))
    )
    for c in range(1, chunks):
        local_ref[c] = local[c] + product(seen[c], pair(states[c - 1]))
        carry_ref[c] = pair(product(seen[c], through[c - 1]))


def opening(width, taps, tails, start_ref, ext_ref):
    made = []
    for index in range(3):
        ext_ref[index, 8 - width : 8, :] = tails[width * index : width * (index + 1)]
        ext_ref[index, 8:, :] = start_ref[8 * index : 8 * index + 8, :]
        made.append(convolved(ext_ref.at[index], 8 - width, 8, taken(index, taps, width)))
    rates = start_ref[24:25, :]
    row = lax.broadcasted_iota(jnp.int32, (8, rates.shape[1]), 0)
    col = lax.broadcasted_iota(jnp.int32, (8, rates.shape[1]), 1)
    strengths = jnp.sum(jnp.where((row == col) & (row < width), rates, 0.0), axis=1, keepdims=True)
    return unit(made[0]), unit(made[1]), made[2], strengths


def finish_kernel(width, small_ref, start_ref, local_ref, carry_ref, memory_ref, out_ref, ext_ref, first_ref):
    depth = local_ref.shape[2]
    later = position(local_ref.shape[0])[1] > 0
    memory = jnp.where(later, memory_ref[:depth, :], 0.0)
    tails = jnp.where(later, memory_ref[depth:, :], 0.0)
    taps = small_ref[...]
    query, key, value, rate = opening(width, taps, tails, start_ref, ext_ref)
    rate = jnp.where(later, rate, 0.0)
    seen = product(pair(jnp.concatenate([key, query], axis=0)), pair(memory))
    delta = rate * (value - seen[:8])
    row = lax.broadcasted_iota(jnp.int32, delta.shape, 0)
    output = seen[8:]
    for t in range(width):
        now = delta[t : t + 1]
        meets = jnp.sum(key * key[t : t + 1], axis=1, keepdims=True)
        delta = jnp.where(row > t, delta - rate * meets * now, delta)
        shown = jnp.sum(query * key[t : t + 1], axis=1, keepdims=True)
        output = jnp.where(row >= t, output + shown * now, output)
    delta = jnp.where(row < width, delta, 0.0)
    turn = (((0,), (0,)), ((), ()))
    key_pair, delta_pair = pair(key), pair(delta)
    both = lax.dot_general(key_pair, delta_pair, turn, preferred_element_type=F32)
    both = both[:depth] + both[depth:]
    memory = pair(memory + both[:, :depth] + both[:, depth:])
    first_ref[...] = output
    gain = small_ref[3 * (width + 1) : 3 * (width + 1) + 1, :]
    for c in range(local_ref.shape[0]):
        output = local_ref[c] + product(carry_ref[c], memory)
        if c == 0:
            tall = lax.broadcasted_iota(jnp.int32, output.shape, 0)
            opened = jnp.concatenate([first_ref[...]] + [jnp.zeros_like(output[8:])], axis=0)
            output = jnp.where((tall < width) & later, opened, output)
        scale = lax.rsqrt(jnp.mean(output * output, axis=-1, keepdims=True) + 1e-05)
        out_ref[c] = (output * scale * gain).astype(BF16)


def unpack_kernel(piece_ref, out_ref):
    depth = piece_ref.shape[2]
    for head in range(piece_ref.shape[0]):
        out_ref[:, head * depth : (head + 1) * depth] = piece_ref[head]


def compose(later, earlier):
    join = functools.partial(jnp.einsum, "ij,jk->ik", precision=lax.Precision.HIGHEST)
    return jnp.stack([join(later[0], earlier[0]), join(later[0], earlier[1]) + later[1]])


def opening_map(width, taps, tails, first):
    made = []
    for index in range(1, 3):
        rows = jnp.concatenate(
            [tails[width * index : width * (index + 1)], first[8 * index : 8 * index + width]]
        )
        own = taken(index, taps, width)
        total = sum(rows[tap : tap + width] * own[tap] for tap in range(width + 1))
        made.append(total / (1.0 + jnp.exp(-total)))
    keys = unit(made[0])
    rates = first[24]
    depth = keys.shape[1]
    maps = jnp.stack([jnp.eye(depth, dtype=F32), jnp.zeros((depth, depth), F32)])
    for t in range(width):
        outer = rates[t] * keys[t][:, None]
        one = jnp.stack([jnp.eye(depth, dtype=F32) - outer * keys[t], outer * made[1][t]])
        maps = compose(one, maps)
    return maps


WHOLE = pl.BlockSpec(memory_space=pltpu.VMEM)
ANY = pl.BlockSpec(memory_space=pl.ANY)


def call(kernel, specs, args, outs, scratch=(), limit=VMEM_LIMIT, out_spec=WHOLE):
    shapes = [jax.ShapeDtypeStruct(shape, dtype) for shape, dtype in outs]
    single = len(shapes) == 1
    return pl.pallas_call(
        kernel,
        out_shape=shapes[0] if single else shapes,
        in_specs=specs,
        out_specs=out_spec if single else [out_spec] * len(shapes),
        scratch_shapes=scratch,
        compiler_params=pltpu.CompilerParams(vmem_limit_bytes=limit),
    )(*args)


def exchange(pieces, count):
    arrived = [pieces[0]]
    for slot in range(1, len(pieces)):
        pairs = [(i, i ^ slot) for i in range(count)]
        arrived.append(lax.ppermute(pieces[slot], "seq", pairs))
    return arrived


def shards(queries, key_rows, value_rows, strength, conv_weight, out_gain):
    taps = conv_weight.shape[1]
    width = taps - 1
    span, heads = strength.shape
    depth = queries.shape[1] // heads
    count = lax.axis_size("seq")
    place = lax.axis_index("seq")
    blocks = count // heads
    assert blocks * heads == count and span == depth and heads & (heads - 1) == 0
    groups = [[b * heads + h for h in range(heads)] for b in range(blocks)]
    block = place // heads

    def share(x):
        return lax.all_to_all(x, "seq", 0, 0, axis_index_groups=groups, tiled=True)

    rows = pltpu.VMEM((span, heads * depth), BF16)
    small = ((16, depth), F32)
    assert 3 * taps < small[0][0]
    packed = call(
        pack_kernel,
        [ANY] * 6,
        (queries, key_rows, value_rows, strength.T, conv_weight, out_gain.reshape(1, depth)),
        [((span + EXTRA, depth), BF16)] * heads + [((2 * span, depth), BF16)] * heads + [small],
        [rows] * 3
        + [pltpu.VMEM((heads, span), F32), pltpu.VMEM(conv_weight.shape, BF16), pltpu.VMEM((1, depth), F32)]
        + [pltpu.VMEM((heads, EXTRA, depth), F32), pltpu.VMEM((heads, EXTRA, depth), BF16), pltpu.VMEM(*small)]
        + [pltpu.SemaphoreType.DMA((6,)), pltpu.SemaphoreType.DMA((4 * heads + 1,))],
        limit=VMEM_PACK,
        out_spec=ANY,
    )
    small = packed[-1]
    keys = exchange(packed[:heads], count)
    pieces = exchange(packed[heads : 2 * heads], count)
    ext = [pltpu.VMEM((heads * span + 8, depth), F32)]
    pairs = ((heads, span, 2 * depth), BF16)
    square = (depth, 2 * depth)
    key, mix, show, factor, opener, edge = call(
        functools.partial(keys_kernel, width),
        [WHOLE] * (1 + heads),
        (small, *keys),
        [pairs] * 3 + [((len(scan_index(heads)), *square), BF16), (square, BF16)]
        + [((24, depth), F32)],
        ext + [pltpu.VMEM((EXTRA * heads, depth), F32), pltpu.VMEM((heads, *square), BF16)],
    )
    final = call(
        functools.partial(state_kernel, width, blocks - 1),
        [WHOLE] * (4 + heads),
        (small, edge, show, factor, *pieces),
        [((depth + 16, depth), F32)],
        ext + [pltpu.VMEM((8 * heads, depth), F32)],
    )
    ring = [(i, (i + heads) % count) for i in range(count)]
    memory = lax.ppermute(final, "seq", ring)
    local, carry, first = call(
        functools.partial(queries_kernel, width),
        [WHOLE] * (7 + heads),
        (small, edge, key, mix, show, opener, factor, *pieces),
        [((heads, span, depth), F32), pairs, ((32, depth), F32)],
        ext * 2,
    )
    if blocks > 2:
        tails = memory[depth:]
        start = jnp.stack([jnp.eye(depth, dtype=F32), jnp.zeros((depth, depth), F32)])

        def joined(x):
            return x[:, :depth].astype(F32) + x[:, depth:].astype(F32)

        join = functools.partial(jnp.matmul, precision=lax.Precision.HIGHEST)
        whole = prefixes(heads, joined(opener), lambda at: joined(factor[at]), join)[-1]
        opened = jnp.where(block > 0, opening_map(width, small, tails, first), start)
        arrived = lax.ppermute(compose(jnp.stack([whole, final[:depth]]), opened), "seq", ring)
        prefix = jnp.where(block > 0, arrived, start)
        reach = 1
        while reach < blocks - 1:
            shift = [(i, (i + reach * heads) % count) for i in range(count)]
            arrived = lax.ppermute(prefix, "seq", shift)
            prefix = jnp.where(block >= reach, compose(prefix, arrived), prefix)
            reach *= 2
        memory = jnp.concatenate([prefix[1], tails])
    mixed = call(
        functools.partial(finish_kernel, width),
        [WHOLE] * 5,
        (small, first, local, carry, memory),
        [((heads, span, depth), BF16)],
        [pltpu.VMEM((3, 16, depth), F32), pltpu.VMEM((8, depth), F32)],
    )
    return call(unpack_kernel, [WHOLE], (share(mixed),), [((span, heads * depth), BF16)])


def solution(mesh):
    placed = (
        P(("groups", "seq"), None),
        P(("groups", "seq"), None),
        P(("groups", "seq"), None),
        P(("groups", "seq"), None),
        P(),
        P(),
    )
    return jax.shard_map(
        shards, mesh=mesh, in_specs=placed, out_specs=P(("groups", "seq"), None), check_vma=False
    )
```
